128 devices in a mesh: gene: 16 (over y, x), samp: 8 (over z, core).
Axes of the slice: x: 4, y: 4, z: 4, core: 2. Of those that a mesh axis runs over, the one named last changes fastest.
Arguments:
- dosage: bfloat16 [12288, 10240], P('gene', 'samp'), may hold values from 0 to 2
- expression: float32 [10240, 32], P('samp', 'gene'), may hold values from -6 to 6
- perms: int32 [128, 10240], P(None, 'samp'), may hold values from 0 to 10239, each once within a row
- windows: int32 [32, 2], P('gene'), may hold values from 0 to 12288, as said below
- order: int32 [32], replicated, may hold values from 0 to 31, each once
Outputs:
- observed: float32 [32], P('gene')
- successive: float32 [32, 128], P('gene')
The draws below stay inside these ranges and needn't reach their ends.
Inputs may be any that keep to these rules, and one draw needn't show every extreme that they name: `windows`: gene i's window [start, end) starts within the 768 variants before the block of variants i // 2 * 768 to (i // 2 + 1) * 768 - 1, or at 0, and ends within the 768 variants after that block, or at 12288; start < end.
All inputs are finite; a program needn't handle non-finite values.
Results may differ from the reference program's by a relative error of at most 0.0015.
Values may be sent and summed in bfloat16 or wider, within the bound.
No kernel may reach another device: no remote copies, remote signals or barrier semaphores. Data moves between devices by JAX's collectives and lax.ppermute only.
A program may use at most 128 MiB of HBM per device.

```python
import jax
import jax.numpy as jnp
from jax import lax

VAR_DEV = 768
GENE_DEV = 2
PERMS = 128
GENES = 32
VARIANTS = 12288
SAMPLES = 10240
N_GENE = 16


def draw_windows(key, part):
    left_key = jax.random.fold_in(key, 11)
    right_key = jax.random.fold_in(key, 23)
    owner = jnp.arange(GENES, dtype=jnp.int32) // GENE_DEV
    before = jax.random.randint(left_key, (GENES,), 1, VAR_DEV + 1, dtype=jnp.int32)
    after = jax.random.randint(right_key, (GENES,), 1, VAR_DEV + 1, dtype=jnp.int32)
    start = jnp.maximum(owner * VAR_DEV - before, 0)
    finish = jnp.minimum((owner + 1) * VAR_DEV + after, VARIANTS)
    return jnp.stack([start, finish], axis=1).astype(jnp.int32)


def block_scale(own_key, shape, cuts, least, largest):
    def one(position, blocks):
        heights = jax.random.uniform(jax.random.fold_in(jax.random.fold_in(own_key, 6), position), (blocks,), jnp.float32, least / len(cuts), largest / len(cuts))
        return jnp.repeat(jnp.exp(heights), shape[position] // blocks).reshape((-1,) + (1,) * (len(shape) - position - 1))

    factor_of = one(*cuts[0])
    for cut in cuts[1:]:
        factor_of = factor_of * one(*cut)
    return factor_of


def normal_values(rng, shape, width, bound, shards=(), kind=jnp.bfloat16):
    drawn = width * jax.random.normal(rng, shape, jnp.float32)
    if shards:
        drawn = drawn * block_scale(rng, shape, shards, -0.22, 0.18)
    return jnp.clip(drawn, -bound, bound).astype(kind)


def setup_inputs(seed: int = 0) -> dict:
    arg_keys = jax.random.split(jax.random.key(seed), 6)
    dosage = jnp.clip(2.0 * jax.random.uniform(arg_keys[0], (VARIANTS, SAMPLES), jnp.float32) ** block_scale(arg_keys[0], (VARIANTS, SAMPLES), ((0, 16), (1, 8)), -0.2, 0.2), 0.0, 2.0).astype(jnp.bfloat16)
    expression = normal_values(arg_keys[1], (SAMPLES, GENES), 1.0, 6.0, ((0, 8), (1, 16)), jnp.float32)
    perms = jax.vmap(lambda own: jax.random.permutation(own, SAMPLES))(jax.random.split(arg_keys[2], PERMS)).reshape((PERMS, SAMPLES)).astype(jnp.int32)
    windows = draw_windows(jax.random.fold_in(arg_keys[5], 71), 0)
    order = jax.random.permutation(arg_keys[4], GENES).astype(jnp.int32)
    return {"dosage": dosage, "expression": expression, "perms": perms, "windows": windows, "order": order}


epsilon = 1e-06

def reference(dosage, expression, perms, windows, order):
    samples = expression.shape[0]
    center = expression - lax.optimization_barrier(jnp.mean(expression, axis=0, keepdims=True))
    scaled = center * lax.rsqrt(lax.optimization_barrier(jnp.mean(center * center, axis=0, keepdims=True)) + epsilon)
    standard = scaled.astype(jnp.bfloat16)
    padded = jnp.pad(dosage, ((VAR_DEV, VAR_DEV), (0, 0)))
    totals = lax.optimization_barrier(jnp.sum(padded.astype(jnp.float32), axis=1))
    squares = lax.optimization_barrier(jnp.sum(jnp.square(padded.astype(jnp.float32)), axis=1))
    row_mean = totals / samples
    row_var = squares / samples - row_mean * row_mean + epsilon
    factor = lax.rsqrt(row_var * samples)

    def one_owner(owner):
        first = owner * VAR_DEV
        block_rows = lax.dynamic_slice_in_dim(padded, first, 3 * VAR_DEV, 0)
        row_scale = lax.dynamic_slice_in_dim(factor, first, 3 * VAR_DEV, 0)
        columns = lax.dynamic_slice_in_dim(standard, (owner * GENE_DEV).astype(jnp.int32), GENE_DEV, 1)
        shuffled = jnp.transpose(columns[perms], (1, 2, 0)).reshape(samples, GENE_DEV * PERMS)
        partial_value = jnp.dot(block_rows, shuffled, preferred_element_type=jnp.float32)
        direct = jnp.dot(block_rows, columns, preferred_element_type=jnp.float32)
        row_index = (first - VAR_DEV + jnp.arange(3 * VAR_DEV, dtype=jnp.int32)).astype(jnp.int32)
        bounds = lax.dynamic_slice_in_dim(windows, (owner * GENE_DEV).astype(jnp.int32), GENE_DEV, 0)
        inside = (row_index[:, None] >= bounds[None, :, 0]) & (row_index[:, None] < bounds[None, :, 1])
        values = jnp.abs(partial_value).reshape(3 * VAR_DEV, GENE_DEV, PERMS) * row_scale[:, None, None]
        maxima = lax.optimization_barrier(jnp.max(jnp.where(inside[:, :, None], values, jnp.float32(0.0)), axis=0))
        seen = lax.optimization_barrier(jnp.max(jnp.where(inside, jnp.abs(direct) * row_scale[:, None], jnp.float32(0.0)), axis=0))
        return (seen, maxima)
    seen, maxima = lax.map(one_owner, jnp.arange(N_GENE, dtype=jnp.int32))
    observed = seen.reshape(GENES)
    ranked = maxima.reshape(GENES, PERMS)[order]
    successive = lax.cummax(ranked, axis=0, reverse=True)
    return (observed, successive)
```

```python
import functools

import jax
import jax.numpy as jnp
from jax import lax
from jax.experimental import pallas as pl
from jax.experimental.pallas import tpu as pltpu
from jax.sharding import Mesh
from jax.sharding import PartitionSpec as P

epsilon = 1e-06
LANES = 128
TILE = 16
HALF = 8
CHUNKS = 2

VM = pl.BlockSpec(memory_space=pltpu.VMEM)
SM = pl.BlockSpec(memory_space=pltpu.SMEM)


def lane_gather(table, index):
    dims = lax.GatherDimensionNumbers(
        offset_dims=(),
        collapsed_slice_dims=(1,),
        start_index_map=(1,),
        operand_batching_dims=(0,),
        start_indices_batching_dims=(0,),
    )
    return lax.gather(
        table,
        index[..., None],
        dims,
        slice_sizes=(1, 1),
        mode=lax.GatherScatterMode.PROMISE_IN_BOUNDS,
    )


def gather_chunk(chunk, place, perms, table, out):
    z, c = place[1], place[2]
    table_rows = table.shape[1]
    tiles = perms.shape[1] // LANES
    group = 5

    def step(t, carry):
        block, part = t // (tiles // group), t % (tiles // group)
        kc, pair = block // 2, block % 2
        first = []
        for k in range(2):
            zz = lax.rem(z + pair * 2 + k, 4)
            cc = lax.rem(c + kc, 2)
            first.append(pl.multiple_of((zz * 2 + cc) * 2 * HALF + chunk * HALF, HALF))
        for u in range(group):
            lane = pl.ds(pl.multiple_of((part * group + u) * LANES, LANES), LANES)
            index = jnp.concatenate([perms[pl.ds(f, HALF), lane] for f in first], axis=0)
            low = (index & (LANES - 1)).astype(jnp.int16)
            high = (index >> 7).astype(jnp.int16)
            found = [jnp.zeros((TILE, LANES), jnp.bfloat16) for _ in range(2)]
            for r in range(table_rows):
                here = high == jnp.int16(r)
                for j in range(2):
                    found[j] = jnp.where(here, lane_gather(table[j, r], low), found[j])
            for j in range(2):
                row = pl.multiple_of(block * 2 * TILE + j * TILE, TILE)
                out[pl.ds(row, TILE), lane] = found[j]
        return carry

    lax.fori_loop(0, 4 * (tiles // group), step, 0)


def first_kernel(place, windows, every, perms, out, table):
    z, c = place[1], place[2]
    shards, genes, width = every.shape
    samples = shards * width
    own = every[z * 2 + c]
    direct = []
    for j in range(genes):
        x = every[:, j, :]
        mean = jnp.sum(x, keepdims=True) / samples
        center = x - mean
        scale = lax.rsqrt(jnp.sum(center * center, keepdims=True) / samples + epsilon)
        scaled = center * scale
        for k in range(shards):
            for i in range(width // LANES):
                piece = scaled[k : k + 1, i * LANES : (i + 1) * LANES]
                table[j, k * (width // LANES) + i] = jnp.broadcast_to(piece, (TILE, LANES)).astype(
                    jnp.bfloat16
                )
        direct.append((own[j : j + 1] - mean) * scale)
    row = lax.broadcasted_iota(jnp.int32, (TILE, width), 0)
    lane = lax.broadcasted_iota(jnp.int32, (TILE, width), 1)
    extra = jnp.where(row == 0, direct[0], jnp.where(row == 1, direct[1], 0.0))
    for j in range(genes):
        for b in range(2):
            w = windows[j, b]
            digits = ((w >> 7).astype(jnp.float32), (w & 127).astype(jnp.float32))
            for d in range(2):
                extra = jnp.where((row == 2 + d) & (lane == j * 2 + b), digits[d], extra)
    extra = jnp.where(row == 4, 1.0, extra)
    out[8 * TILE : 9 * TILE, :] = extra.astype(jnp.bfloat16)
    gather_chunk(0, place, perms, table, out)


def later_kernel(chunk, place, perms, table, out):
    gather_chunk(chunk, place, perms, table, out)


def times(rows, dosage):
    return lax.dot_general(
        rows, dosage, (((1,), (1,)), ((), ())), preferred_element_type=jnp.float32
    )


def product_kernel(with_stats, left, own, right, dosage, keep, send, *win):
    weights = dosage[...]
    small = []
    for o, ref in enumerate((left, own, right)):
        got = times(ref[: 8 * TILE, :], weights)
        for kc, dst in ((0, keep), (1, send)):
            for kz in range(4):
                for j in range(2):
                    src = kc * 64 + (kz // 2) * 32 + j * TILE + (kz % 2) * HALF
                    to = kz * 48 + (o * 2 + j) * HALF
                    dst[to : to + HALF, :] = got[src : src + HALF]
        if with_stats:
            small.append(times(ref[8 * TILE :, :], weights))
    if with_stats:
        variants, width = dosage.shape
        total = jnp.zeros((variants, LANES), jnp.float32)
        for i in range(width // LANES):
            d = dosage[:, i * LANES : (i + 1) * LANES].astype(jnp.float32)
            total = total + d * d
        squares = lax.dot_general(
            jnp.ones((8, LANES), jnp.float32),
            total,
            (((1,), (1,)), ((), ())),
            precision=lax.Precision.HIGHEST,
            preferred_element_type=jnp.float32,
        )
        stats = jnp.concatenate(
            [small[0][:2], small[1][:2], small[2][:2], small[1][4:5], squares[:1]], axis=0
        )
        keep[192:200, :] = stats
        send[192:200, :] = stats
        win_ref = win[0]
        win_ref[...] = jnp.zeros_like(win_ref)
        for o, ref in enumerate((left, own, right)):
            e = ref[8 * TILE :, :LANES].astype(jnp.float32)
            win_ref[o : o + 1, :] = e[2:3] * 128.0 + e[3:4]


def split_kernel(keep, got, *outs):
    for kz, out in enumerate(outs):
        out[:48, :] = keep[kz * 48 : kz * 48 + 48, :] + got[kz * 48 : kz * 48 + 48, :]
        if out.shape[0] > 48:
            out[48:, :] = keep[192:200, :] + got[192:200, :]


def maxima_kernel(samples, place, win, *refs):
    refs, out = refs[:-1], refs[-1]
    chunks = []
    for h in range(CHUNKS):
        part = refs[4 * h : 4 * h + 4]
        chunks.append((part[0][...] + part[1][...]) + (part[2][...] + part[3][...]))
    stats = chunks[0][48:56]
    mean = stats[6:7] / samples
    spread = stats[7:8] / samples - mean * mean + epsilon
    scale = lax.rsqrt(spread * samples)
    variants = scale.shape[1]
    index = lax.broadcasted_iota(jnp.int32, (1, variants), 1) + place[0] * variants
    index = index.astype(jnp.float32)
    lane = lax.broadcasted_iota(jnp.int32, (HALF, LANES), 1)
    tile = jnp.zeros((HALF, LANES), jnp.float32)
    direct = jnp.abs(stats) * scale
    for o in range(3):
        for j in range(2):
            n = o * 2 + j
            lo = win[o : o + 1, j * 2 : j * 2 + 1]
            hi = win[o : o + 1, j * 2 + 1 : j * 2 + 2]
            factor = (index >= lo) & (index < hi)
            for h in range(CHUNKS):
                v = jnp.abs(chunks[h][n * HALF : n * HALF + HALF]) * scale
                best = jnp.max(jnp.where(factor, v, 0.0), axis=1, keepdims=True)
                tile = jnp.where(lane == h * 6 + n, best, tile)
            best = jnp.max(jnp.where(factor, direct[n : n + 1], 0.0), axis=1, keepdims=True)
            tile = jnp.where(lane == 12 + n, best, tile)
    for i in range(out.shape[0]):
        out[i] = tile


def rank_kernel(place, order, blocks, out, observed, store):
    owners = blocks.shape[0]
    for o in range(owners):
        best = blocks[o]
        if o > 0:
            best = jnp.maximum(best, pltpu.roll(blocks[o - 1], LANES - 2, 1))
        if o < owners - 1:
            best = jnp.maximum(best, pltpu.roll(blocks[o + 1], 2, 1))
        store[2 * o] = best
        store[2 * o + 1] = pltpu.roll(best, LANES - 1, 1)
    g = place[0]
    zero = jnp.zeros((HALF, LANES), jnp.float32)
    tails = [zero, zero]
    for i in range(2 * owners):
        value = store[order[i]]
        for k in range(2):
            tails[k] = jnp.where(i >= 2 * g + k, jnp.maximum(tails[k], value), tails[k])
    lane = lax.broadcasted_iota(jnp.int32, (HALF, LANES), 1)
    tile = zero
    for k in range(2):
        for h in range(CHUNKS):
            tile = jnp.where(lane == 2 * k + h, tails[k][:, h * 6 + 2 : h * 6 + 3], tile)
    for i in range(out.shape[0]):
        out[i] = tile
    own = store[2 * g]
    observed[...] = jnp.concatenate([own[:1, 14:15], own[:1, 15:16]], axis=1)


def final_kernel(parts, out):
    lane = lax.broadcasted_iota(jnp.int32, (HALF, LANES), 1)
    row = lax.broadcasted_iota(jnp.int32, (HALF, LANES), 0)
    for k in range(2):
        spread = jnp.zeros((HALF, LANES), jnp.float32)
        for d in range(parts.shape[0]):
            for h in range(CHUNKS):
                column = parts[d, :, 2 * k + h : 2 * k + h + 1]
                spread = jnp.where(lane // HALF == d * 2 + h, column, spread)
        out[k : k + 1, :] = jnp.sum(
            jnp.where(lane % HALF == row, spread, 0.0), axis=0, keepdims=True
        )


def shape(dims, kind=jnp.float32):
    return jax.ShapeDtypeStruct(dims, kind)


def on_device(dosage, expression, perms, windows, order):
    variants, width = dosage.shape
    owners = lax.axis_size("gene")
    shards = 8
    samples = width * shards
    g, z, c = lax.axis_index("gene"), lax.axis_index("z"), lax.axis_index("core")
    place = jnp.stack([g, z, c]).astype(jnp.int32)
    copies = jnp.broadcast_to(expression.T[None], (shards, 2, width))
    every = lax.all_to_all(copies, ("z", "core"), 0, 0, tiled=True)

    table_shape = shape((2, samples // LANES, TILE, LANES), jnp.bfloat16)
    first, table = pl.pallas_call(
        first_kernel,
        out_shape=(shape((9 * TILE, width), jnp.bfloat16), table_shape),
        in_specs=[SM, SM, VM, VM],
        out_specs=(VM, VM),
        name="first_gather",
    )(place, windows, every, perms)
    shuffled = [first]
    for h in range(1, CHUNKS):
        shuffled.append(
            pl.pallas_call(
                functools.partial(later_kernel, h),
                out_shape=shape((8 * TILE, width), jnp.bfloat16),
                in_specs=[SM, VM, VM],
                out_specs=VM,
                name="later_gather",
            )(place, perms, table)
        )
    ahead = [(i, (i + 1) % owners) for i in range(owners)]
    back = [(b, a) for a, b in ahead]
    sums = []
    for h, own in enumerate(shuffled):
        left = lax.ppermute(own, "gene", ahead)
        right = lax.ppermute(own, "gene", back)
        rows = 200 if h == 0 else 192
        outs = [shape((rows, variants)), shape((rows, variants))]
        if h == 0:
            outs.append(shape((8, LANES)))
        made = pl.pallas_call(
            functools.partial(product_kernel, h == 0),
            out_shape=tuple(outs),
            in_specs=[VM] * 4,
            out_specs=tuple([VM] * len(outs)),
            name="products",
        )(left, own, right, dosage)
        if h == 0:
            win = made[2]
        keep, send = made[:2]
        got = lax.ppermute(send, "core", [(0, 1), (1, 0)])
        depth = 56 if h == 0 else 48
        parts = pl.pallas_call(
            split_kernel,
            out_shape=tuple([shape((depth, variants))] * 4),
            in_specs=[VM] * 2,
            out_specs=tuple([VM] * 4),
            name="split",
        )(keep, got)
        sums.append(parts[0])
        for k in range(1, 4):
            sums.append(lax.ppermute(parts[k], "z", [(i, (i + k) % 4) for i in range(4)]))
    tiles = pl.pallas_call(
        functools.partial(maxima_kernel, samples),
        out_shape=shape((owners, HALF, LANES)),
        in_specs=[SM] + [VM] * (1 + len(sums)),
        out_specs=VM,
        name="maxima",
    )(place, win, *sums)
    tiles = lax.all_to_all(tiles, "gene", 0, 0, tiled=True)
    tails, observed = pl.pallas_call(
        rank_kernel,
        out_shape=(shape((shards, HALF, LANES)), shape((1, 2))),
        in_specs=[SM, SM, VM],
        out_specs=(VM, VM),
        scratch_shapes=[pltpu.VMEM((2 * owners, HALF, LANES), jnp.float32)],
        name="rank",
    )(place, order, tiles)
    tails = lax.all_to_all(tails, ("z", "core"), 0, 0, tiled=True)
    successive = pl.pallas_call(
        final_kernel, out_shape=shape((2, LANES)), in_specs=[VM], out_specs=VM, name="final"
    )(tails)
    return observed.reshape(2), successive


def solution(mesh):
    split = Mesh(mesh.devices.reshape(16, 4, 2), ("gene", "z", "core"))
    samp = ("z", "core")
    placed = (P("gene", samp), P(samp, "gene"), P(None, samp), P("gene", None), P())
    return jax.shard_map(
        on_device,
        mesh=split,
        in_specs=placed,
        out_specs=(P("gene"), P("gene", None)),
        check_vma=False,
    )
```

```python
import functools

import jax
import jax.numpy as jnp
from jax import lax
from jax.experimental import pallas as pl
from jax.experimental.pallas import tpu as pltpu
from jax.sharding import Mesh
from jax.sharding import PartitionSpec as P


epsilon = 1e-06
LANES = 128
TILE = 16
HALF = 8
CHUNKS = 2

VM = pl.BlockSpec(memory_space=pltpu.VMEM)
SM = pl.BlockSpec(memory_space=pltpu.SMEM)


def lane_gather(table, index):
    dims = lax.GatherDimensionNumbers(
        offset_dims=(),
        collapsed_slice_dims=(1,),
        start_index_map=(1,),
        operand_batching_dims=(0,),
        start_indices_batching_dims=(0,),
    )
    return lax.gather(
        table,
        index[..., None],
        dims,
        slice_sizes=(1, 1),
        mode=lax.GatherScatterMode.PROMISE_IN_BOUNDS,
    )


def gather_chunk(chunk, place, perms, table, out):
    z, c = place[1], place[2]
    table_rows = table.shape[1]
    tiles = perms.shape[1] // LANES
    group = 5

    def step(t, carry):
        block, part = t // (tiles // group), t % (tiles // group)
        kc, pair = block // 2, block % 2
        first = []
        for k in range(2):
            zz = lax.rem(z + pair * 2 + k, 4)
            cc = lax.rem(c + kc, 2)
            first.append(pl.multiple_of((zz * 2 + cc) * 2 * HALF + chunk * HALF, HALF))
        for u in range(group):
            lane = pl.ds(pl.multiple_of((part * group + u) * LANES, LANES), LANES)
            index = jnp.concatenate([perms[pl.ds(f, HALF), lane] for f in first], axis=0)
            low = (index & (LANES - 1)).astype(jnp.int16)
            high = (index >> 7).astype(jnp.int16)
            found = [jnp.zeros((TILE, LANES), jnp.bfloat16) for _ in range(2)]
            for r in range(table_rows):
                here = high == jnp.int16(r)
                for j in range(2):
                    found[j] = jnp.where(here, lane_gather(table[j, r], low), found[j])
            for j in range(2):
                row = pl.multiple_of(block * 2 * TILE + j * TILE, TILE)
                out[pl.ds(row, TILE), lane] = found[j]
        return carry

    lax.fori_loop(0, 4 * (tiles // group), step, 0)


def first_kernel(place, windows, every, perms, out, table):
    z, c = place[1], place[2]
    shards, genes, width = every.shape
    samples = shards * width
    own = every[z * 2 + c]
    direct = []
    for j in range(genes):
        x = every[:, j, :]
        mean = jnp.sum(x, keepdims=True) / samples
        center = x - mean
        scale = lax.rsqrt(jnp.sum(center * center, keepdims=True) / samples + epsilon)
        scaled = center * scale
        for k in range(shards):
            for i in range(width // LANES):
                piece = scaled[k : k + 1, i * LANES : (i + 1) * LANES]
                table[j, k * (width // LANES) + i] = jnp.broadcast_to(piece, (TILE, LANES)).astype(
                    jnp.bfloat16
                )
        direct.append((own[j : j + 1] - mean) * scale)
    row = lax.broadcasted_iota(jnp.int32, (TILE, width), 0)
    lane = lax.broadcasted_iota(jnp.int32, (TILE, width), 1)
    extra = jnp.where(row == 0, direct[0], jnp.where(row == 1, direct[1], 0.0))
    for j in range(genes):
        for b in range(2):
            w = windows[j, b]
            digits = ((w >> 7).astype(jnp.float32), (w & 127).astype(jnp.float32))
            for d in range(2):
                extra = jnp.where((row == 2 + d) & (lane == j * 2 + b), digits[d], extra)
    extra = jnp.where(row == 4, 1.0, extra)
    out[8 * TILE : 9 * TILE, :] = extra.astype(jnp.bfloat16)
    gather_chunk(0, place, perms, table, out)


def later_kernel(chunk, place, perms, table, out):
    gather_chunk(chunk, place, perms, table, out)


def times(rows, dosage):
    return lax.dot_general(
        rows, dosage, (((1,), (1,)), ((), ())), preferred_element_type=jnp.float32
    )


def squares_kernel(dosage, out):
    variants, width = dosage.shape
    total = jnp.zeros((variants, LANES), jnp.float32)
    for i in range(width // LANES):
        d = dosage[:, i * LANES : (i + 1) * LANES].astype(jnp.float32)
        total = total + d * d
    out[...] = lax.dot_general(
        jnp.ones((8, LANES), jnp.float32),
        total,
        (((1,), (1,)), ((), ())),
        precision=lax.Precision.HIGHEST,
        preferred_element_type=jnp.float32,
    )


def product_kernel(with_stats, left, own, right, dosage, *refs):
    if with_stats:
        squares, keep, send, win_ref = refs
    else:
        keep, send = refs
    weights = dosage[...]
    small = []
    for o, ref in enumerate((left, own, right)):
        got = times(ref[: 8 * TILE, :], weights)
        for kc, dst in ((0, keep), (1, send)):
            for kz in range(4):
                for j in range(2):
                    src = kc * 64 + (kz // 2) * 32 + j * TILE + (kz % 2) * HALF
                    to = kz * 48 + (o * 2 + j) * HALF
                    dst[to : to + HALF, :] = got[src : src + HALF]
        if with_stats:
            small.append(times(ref[8 * TILE :, :], weights))
    if with_stats:
        stats = jnp.concatenate(
            [small[0][:2], small[1][:2], small[2][:2], small[1][4:5], squares[:1]], axis=0
        )
        keep[192:200, :] = stats
        send[192:200, :] = stats
        win_ref[...] = jnp.zeros_like(win_ref)
        for o, ref in enumerate((left, own, right)):
            e = ref[8 * TILE :, :LANES].astype(jnp.float32)
            win_ref[o : o + 1, :] = e[2:3] * 128.0 + e[3:4]


def split_kernel(keep, got, *outs):
    for kz, out in enumerate(outs):
        out[:48, :] = keep[kz * 48 : kz * 48 + 48, :] + got[kz * 48 : kz * 48 + 48, :]
        if out.shape[0] > 48:
            out[48:, :] = keep[192:200, :] + got[192:200, :]


def maxima_kernel(samples, place, win, *refs):
    refs, out = refs[:-1], refs[-1]
    chunks = []
    for h in range(CHUNKS):
        part = refs[4 * h : 4 * h + 4]
        chunks.append((part[0][...] + part[1][...]) + (part[2][...] + part[3][...]))
    stats = chunks[0][48:56]
    mean = stats[6:7] / samples
    spread = stats[7:8] / samples - mean * mean + epsilon
    scale = lax.rsqrt(spread * samples)
    variants = scale.shape[1]
    index = lax.broadcasted_iota(jnp.int32, (1, variants), 1) + place[0] * variants
    index = index.astype(jnp.float32)
    lane = lax.broadcasted_iota(jnp.int32, (HALF, LANES), 1)
    tile = jnp.zeros((HALF, LANES), jnp.float32)
    direct = jnp.abs(stats) * scale
    row = lax.broadcasted_iota(jnp.int32, (HALF, LANES), 0)
    seen = []
    for o in range(3):
        for j in range(2):
            n = o * 2 + j
            lo = win[o : o + 1, j * 2 : j * 2 + 1]
            hi = win[o : o + 1, j * 2 + 1 : j * 2 + 2]
            inside = (index >= lo) & (index < hi)
            for h in range(CHUNKS):
                v = jnp.abs(chunks[h][n * HALF : n * HALF + HALF]) * scale
                best = jnp.max(jnp.where(inside, v, 0.0), axis=1, keepdims=True)
                tile = jnp.where(lane // HALF == n * CHUNKS + h, best, tile)
            seen.append(
                jnp.max(jnp.where(inside, direct[n : n + 1], 0.0), axis=1, keepdims=True)
            )
    line = jnp.sum(jnp.where(lane % HALF == row, tile, 0.0), axis=0, keepdims=True)
    for n in range(6):
        line = jnp.where(lane[:1] == 96 + n, seen[n], line)
    for i in range(out.shape[0] // HALF):
        out[i * HALF : (i + 1) * HALF, :] = jnp.broadcast_to(line, (HALF, LANES))


def final_kernel(place, order, parts, out, observed, store):
    shards = HALF
    owners = parts.shape[0] // shards
    block = lambda o: parts[o * shards : (o + 1) * shards, :]
    width = 2 * HALF
    for o in range(owners):
        best = block(o)
        if o > 0:
            best = jnp.maximum(best, pltpu.roll(block(o - 1), LANES - 2 * width, 1))
        if o < owners - 1:
            best = jnp.maximum(best, pltpu.roll(block(o + 1), 2 * width, 1))
        store[2 * o] = best
        store[2 * o + 1] = pltpu.roll(best, LANES - width, 1)
    g = place[0]
    zero = jnp.zeros((shards, LANES), jnp.float32)
    tails = [zero, zero]
    for i in range(2 * owners):
        value = store[order[i]]
        for k in range(2):
            tails[k] = jnp.where(i >= 2 * g + k, jnp.maximum(tails[k], value), tails[k])
    lane = lax.broadcasted_iota(jnp.int32, (shards, LANES), 1)
    row = lax.broadcasted_iota(jnp.int32, (shards, LANES), 0)
    for k in range(2):
        moved = pltpu.roll(tails[k], LANES - 2 * width, 1)
        moved = pltpu.roll(moved, 0, 1, stride=width, stride_axis=0)
        out[k : k + 1, :] = jnp.sum(
            jnp.where(lane // width == row, moved, 0.0), axis=0, keepdims=True
        )
    part = lambda o: parts[pl.ds(pl.multiple_of(o * shards, shards), shards), :][:1]
    seen = part(g)
    left = pltpu.roll(part(jnp.maximum(g - 1, 0)), LANES - 2, 1)
    right = pltpu.roll(part(jnp.minimum(g + 1, owners - 1)), 2, 1)
    seen = jnp.maximum(seen, jnp.where(g > 0, left, 0.0))
    seen = jnp.maximum(seen, jnp.where(g < owners - 1, right, 0.0))
    observed[...] = seen[:, 98:100]


def call(kernel, outs, args, us, scratch=()):
    scalar = [a.size <= 64 for a in args]
    many = isinstance(outs, list)
    made = pl.pallas_call(
        kernel,
        out_shape=tuple(outs) if many else outs,
        in_specs=[SM if k else VM for k in scalar],
        out_specs=tuple([VM] * len(outs)) if many else VM,
        scratch_shapes=scratch,
        compiler_params=pltpu.CompilerParams(vmem_limit_bytes=24 << 20),
        cost_estimate=pl.CostEstimate(flops=int(us * 1e9), bytes_accessed=0, transcendentals=0),
    )
    args = [
        a if k else pltpu.with_memory_space_constraint(a, pltpu.VMEM)
        for a, k in zip(args, scalar)
    ]
    return made(*args)


def shape(dims, kind=jnp.float32):
    return pltpu.VMEM(dims, kind)


def on_device(dosage, expression, perms, windows, order):
    variants, width = dosage.shape
    owners = lax.axis_size("gene")
    shards = 8
    samples = width * shards
    g, z, c = lax.axis_index("gene"), lax.axis_index("z"), lax.axis_index("core")
    place = jnp.stack([g, z, c]).astype(jnp.int32)
    copies = jnp.broadcast_to(expression.T[None], (shards, 2, width))
    every = lax.all_to_all(copies, ("z", "core"), 0, 0, tiled=True)

    squares = call(squares_kernel, shape((8, variants)), [dosage], 1)
    table_shape = shape((2, samples // LANES, TILE, LANES), jnp.bfloat16)
    first, table = call(
        first_kernel,
        [shape((9 * TILE, width), jnp.bfloat16), table_shape],
        [place, windows, every, perms],
        9,
    )
    shuffled = [first]
    for h in range(1, CHUNKS):
        shuffled.append(
            call(
                functools.partial(later_kernel, h),
                shape((8 * TILE, width), jnp.bfloat16),
                [place, perms, table],
                9,
            )
        )
    ahead = [(i, (i + 1) % owners) for i in range(owners)]
    back = [(b, a) for a, b in ahead]
    sums = []
    for h, own in enumerate(shuffled):
        left = lax.ppermute(own, "gene", ahead)
        right = lax.ppermute(own, "gene", back)
        rows = 200 if h == 0 else 192
        outs = [shape((rows, variants)), shape((rows, variants))]
        args = [left, own, right, dosage]
        if h == 0:
            outs.append(shape((8, LANES)))
            args.append(squares)
        made = call(functools.partial(product_kernel, h == 0), outs, args, 4)
        if h == 0:
            win = made[2]
        keep, send = made[:2]
        got = lax.ppermute(send, "core", [(0, 1), (1, 0)])
        depth = 56 if h == 0 else 48
        parts = call(split_kernel, [shape((depth, variants))] * 4, [keep, got], 1)
        sums.append(parts[0])
        for k in range(1, 4):
            sums.append(lax.ppermute(parts[k], "z", [(i, (i + k) % 4) for i in range(4)]))
    everyone = owners * shards
    lines = call(
        functools.partial(maxima_kernel, samples), shape((everyone, LANES)), [place, win, *sums], 2
    )
    lines = lax.all_to_all(
        lines.reshape(everyone, 1, LANES), ("gene", "z", "core"), 0, 0, tiled=True
    ).reshape(everyone, LANES)
    successive, observed = call(
        final_kernel,
        [shape((2, LANES)), shape((1, 2))],
        [place, order, lines],
        2,
        [pltpu.VMEM((2 * owners, HALF, LANES), jnp.float32)],
    )
    return observed.reshape(2), successive


def solution(mesh):
    split = Mesh(mesh.devices.reshape(16, 4, 2), ("gene", "z", "core"))
    samp = ("z", "core")
    placed = (P("gene", samp), P(samp, "gene"), P(None, samp), P("gene", None), P())
    return jax.shard_map(
        on_device,
        mesh=split,
        in_specs=placed,
        out_specs=(P("gene"), P("gene", None)),
        check_vma=False,
    )
```

```python
import functools

import jax
import jax.numpy as jnp
from jax import lax
from jax.experimental import pallas as pl
from jax.experimental.pallas import tpu as pltpu
from jax.sharding import Mesh
from jax.sharding import PartitionSpec as P


epsilon = 1e-06
LANES = 128
TILE = 16
HALF = 8
CHUNKS = 2

VM = pl.BlockSpec(memory_space=pltpu.VMEM)
SM = pl.BlockSpec(memory_space=pltpu.SMEM)


def lane_gather(table, index):
    dims = lax.GatherDimensionNumbers(
        offset_dims=(),
        collapsed_slice_dims=(1,),
        start_index_map=(1,),
        operand_batching_dims=(0,),
        start_indices_batching_dims=(0,),
    )
    return lax.gather(
        table,
        index[..., None],
        dims,
        slice_sizes=(1, 1),
        mode=lax.GatherScatterMode.PROMISE_IN_BOUNDS,
    )


def gather_chunk(chunk, place, perms, table, out):
    z, c = place[1], place[2]
    table_rows = table.shape[1]
    tiles = perms.shape[1] // LANES
    group = 5

    def step(t, carry):
        block, part = t // (tiles // group), t % (tiles // group)
        kc, pair = block // 2, block % 2
        first = []
        for k in range(2):
            zz = lax.rem(z + pair * 2 + k, 4)
            cc = lax.rem(c + kc, 2)
            first.append(pl.multiple_of((zz * 2 + cc) * 2 * HALF + chunk * HALF, HALF))
        for u in range(group):
            lane = pl.ds(pl.multiple_of((part * group + u) * LANES, LANES), LANES)
            index = jnp.concatenate([perms[pl.ds(f, HALF), lane] for f in first], axis=0)
            low = (index & (LANES - 1)).astype(jnp.int16)
            high = (index >> 7).astype(jnp.int16)
            found = [jnp.zeros((TILE, LANES), jnp.bfloat16) for _ in range(2)]
            for r in range(table_rows):
                here = high == jnp.int16(r)
                for j in range(2):
                    found[j] = jnp.where(here, lane_gather(table[j, r], low), found[j])
            for j in range(2):
                row = pl.multiple_of(block * 2 * TILE + j * TILE, TILE)
                out[pl.ds(row, TILE), lane] = found[j]
        return carry

    lax.fori_loop(0, 4 * (tiles // group), step, 0)


def lane_sums(rows):
    return lax.dot_general(
        jnp.ones((8, LANES), jnp.float32),
        rows,
        (((1,), (1,)), ((), ())),
        precision=lax.Precision.HIGHEST,
        preferred_element_type=jnp.float32,
    )[:1]


def pack_kernel(dosage, expression, out, kept, levels, done):
    shards, _, _ = out.shape
    variants, width = dosage.shape
    pieces = variants // LANES
    copies = []
    for i in range(pieces):
        rows = pl.ds(i * LANES, LANES)
        copies.append(pltpu.make_async_copy(dosage.at[rows], kept.at[rows], done.at[i]))
        copies[-1].start()
    fetch = pltpu.make_async_copy(expression, levels, done.at[pieces])
    fetch.start()
    for i in range(pieces):
        copies[i].wait()
        total = jnp.zeros((LANES, LANES), jnp.float32)
        square = jnp.zeros((LANES, LANES), jnp.float32)
        for k in range(width // LANES):
            v = kept[i * LANES : (i + 1) * LANES, k * LANES : (k + 1) * LANES].astype(jnp.float32)
            total = total + v
            square = square + v * v
        for j, moment in enumerate((lane_sums(total), lane_sums(square))):
            for d in range(shards):
                out[d, j : j + 1, width + i * LANES : width + (i + 1) * LANES] = moment
    fetch.wait()
    for d in range(shards):
        out[d, :, :width] = levels[...]


def first_kernel(variants, place, windows, every, perms, out, table, stat):
    z, c = place[1], place[2]
    shards, genes, wide = every.shape
    width = wide - variants
    samples = shards * width
    moments = jnp.sum(every[:, :, width:], axis=0)
    row_mean = moments[0:1] / samples
    spread = moments[1:2] / samples - row_mean * row_mean + epsilon
    stat[...] = jnp.zeros_like(stat)
    stat[0:1, :] = row_mean
    stat[1:2, :] = lax.rsqrt(spread * samples)
    own = every[z * 2 + c][:, :width]
    direct, sums = [], []
    for j in range(genes):
        x = every[:, j, :width]
        mean = jnp.sum(x, keepdims=True) / samples
        center = x - mean
        scale = lax.rsqrt(jnp.sum(center * center, keepdims=True) / samples + epsilon)
        scaled = (center * scale).astype(jnp.bfloat16).astype(jnp.float32)
        sums.append(jnp.sum(scaled, keepdims=True))
        for k in range(shards):
            for i in range(width // LANES):
                piece = scaled[k : k + 1, i * LANES : (i + 1) * LANES]
                table[j, k * (width // LANES) + i] = jnp.broadcast_to(piece, (TILE, LANES)).astype(
                    jnp.bfloat16
                )
        direct.append((own[j : j + 1] - mean) * scale)
    row = lax.broadcasted_iota(jnp.int32, (TILE, width), 0)
    lane = lax.broadcasted_iota(jnp.int32, (TILE, width), 1)
    extra = jnp.where(row == 0, direct[0], jnp.where(row == 1, direct[1], 0.0))
    for j in range(genes):
        for b in range(2):
            w = windows[j, b]
            digits = ((w >> 7).astype(jnp.float32), (w & 127).astype(jnp.float32))
            for d in range(2):
                extra = jnp.where((row == 2 + d) & (lane == j * 2 + b), digits[d], extra)
        rest = sums[j]
        for d in range(3):
            digit = rest.astype(jnp.bfloat16).astype(jnp.float32)
            rest = rest - digit
            extra = jnp.where((row == 4 + d) & (lane == j), digit, extra)
    out[8 * TILE : 9 * TILE, :] = extra.astype(jnp.bfloat16)
    gather_chunk(0, place, perms, table, out)


def later_kernel(chunk, place, perms, table, out):
    gather_chunk(chunk, place, perms, table, out)


def times(rows, dosage):
    return lax.dot_general(
        rows, dosage, (((1,), (1,)), ((), ())), preferred_element_type=jnp.float32
    )


def product_kernel(kc, with_direct, left, own, right, dosage, stat, *outs):
    blocks = [ref[kc * 4 * TILE : (kc + 1) * 4 * TILE, :] for ref in (left, own, right)]
    if with_direct:
        blocks += [ref[8 * TILE :, :] for ref in (left, own, right)]
    rows = jnp.concatenate(blocks, axis=0)
    mean, scale = stat[0:1, :], stat[1:2, :]
    got = (times(rows, dosage[...]) - jnp.sum(rows.astype(jnp.float32), axis=1, keepdims=True) * mean) * scale
    out = outs[0]
    for o in range(3):
        for kz in range(4):
            for j in range(2):
                src = o * 4 * TILE + (kz // 2) * 2 * TILE + j * TILE + (kz % 2) * HALF
                to = kz * 48 + (o * 2 + j) * HALF
                out[to : to + HALF, :] = got[src : src + HALF]
    if with_direct:
        first = 12 * TILE
        zero = jnp.zeros((2, got.shape[1]), jnp.float32)
        out[192:200, :] = jnp.concatenate(
            [got[first + o * TILE : first + o * TILE + 2] for o in range(3)] + [zero], axis=0
        )
        info = outs[1]
        info[...] = jnp.zeros_like(info)
        lane = lax.broadcasted_iota(jnp.int32, (1, LANES), 1)
        for o, ref in enumerate((left, own, right)):
            e = ref[8 * TILE :, :LANES].astype(jnp.float32)
            line = jnp.where(lane < 4, e[2:3] * 128.0 + e[3:4], 0.0)
            total = (e[4:5] + e[5:6]) + e[6:7]
            for j in range(2):
                line = jnp.where(lane == 4 + j, total[:, j : j + 1], line)
            info[o : o + 1, :] = line


LEVELS = 32767.0
PARTS = 256.0


def bound_code(largest):
    return jnp.clip(jnp.ceil(largest * PARTS), 1.0, LEVELS)


def coded(values, code):
    scaled = values * (LEVELS * PARTS / code)
    return jnp.clip(jnp.round(scaled), -LEVELS, LEVELS)


def to_int16(values):
    return values.astype(jnp.int32).astype(jnp.int16)


def split_kernel(keep0, send0, got0, keep1, got1, own, *refs):
    messages, hold = refs[:3], refs[3]
    largest = jnp.zeros((HALF, own.shape[1]), jnp.float32)
    for kz in range(4):
        for h, (keep, got) in enumerate(((keep0, got0), (keep1, got1))):
            for t in range(6):
                at = kz * 48 + t * HALF
                v = keep[at : at + HALF, :] + got[at : at + HALF, :]
                to = h * 48 + t * HALF
                if kz == 0:
                    own[to : to + HALF, :] = v
                else:
                    hold[kz - 1, to : to + HALF, :] = v
                    largest = jnp.maximum(largest, jnp.abs(v))
    direct = send0[192:200, :] + got0[192:200, :]
    own[96:104, :] = direct
    codes = [bound_code(jnp.max(v, keepdims=True)) for v in (largest, jnp.abs(direct))]
    row = lax.broadcasted_iota(jnp.int32, direct.shape, 0)
    tail = jnp.where(row == 0, codes[0], jnp.where(row == 1, codes[1], 0.0))
    tail = to_int16(jnp.concatenate([coded(direct, codes[1]), tail], axis=0))
    for k, message in enumerate(messages):
        for t in range(6):
            rows = slice(t * TILE, (t + 1) * TILE)
            message[rows, :] = to_int16(coded(hold[k, rows, :], codes[0]))
        message[96:112, :] = tail


def maxima_kernel(place, info, stat, own, *refs):
    messages, out = refs[:3], refs[3]
    values, direct = own[:96, :], own[96:104, :]
    for message in messages:
        tail = message[96:112, :].astype(jnp.int32).astype(jnp.float32)
        unit = 1.0 / (LEVELS * PARTS)
        values = values + message[:96, :].astype(jnp.int32).astype(jnp.float32) * (tail[8:9] * unit)
        direct = direct + tail[:8] * (tail[9:10] * unit)
    offset = stat[0:1, :] * stat[1:2, :]
    variants = offset.shape[1]
    index = lax.broadcasted_iota(jnp.int32, (1, variants), 1) + place[0] * variants
    index = index.astype(jnp.float32)
    lane = lax.broadcasted_iota(jnp.int32, (HALF, LANES), 1)
    row = lax.broadcasted_iota(jnp.int32, (HALF, LANES), 0)
    tile = jnp.zeros((HALF, LANES), jnp.float32)
    seen = []
    for o in range(3):
        for j in range(2):
            n = o * 2 + j
            lo = info[o : o + 1, j * 2 : j * 2 + 1]
            hi = info[o : o + 1, j * 2 + 1 : j * 2 + 2]
            back = offset * info[o : o + 1, 4 + j : 5 + j]
            inside = (index >= lo) & (index < hi)
            for h in range(CHUNKS):
                at = h * 48 + n * HALF
                v = jnp.abs(values[at : at + HALF] + back)
                best = jnp.max(jnp.where(inside, v, 0.0), axis=1, keepdims=True)
                tile = jnp.where(lane // HALF == n * CHUNKS + h, best, tile)
            v = jnp.abs(direct[n : n + 1] + back)
            seen.append(jnp.max(jnp.where(inside, v, 0.0), axis=1, keepdims=True))
    line = jnp.sum(jnp.where(lane % HALF == row, tile, 0.0), axis=0, keepdims=True)
    for n in range(6):
        line = jnp.where(lane[:1] == 96 + n, seen[n], line)
    for i in range(out.shape[0] // HALF):
        out[i * HALF : (i + 1) * HALF, :] = jnp.broadcast_to(line, (HALF, LANES))


def final_kernel(place, order, parts, out, observed, store):
    shards = HALF
    owners = parts.shape[0] // shards
    block = lambda o: parts[o * shards : (o + 1) * shards, :]
    width = 2 * HALF
    for o in range(owners):
        best = block(o)
        if o > 0:
            best = jnp.maximum(best, pltpu.roll(block(o - 1), LANES - 2 * width, 1))
        if o < owners - 1:
            best = jnp.maximum(best, pltpu.roll(block(o + 1), 2 * width, 1))
        store[2 * o] = best
        store[2 * o + 1] = pltpu.roll(best, LANES - width, 1)
    g = place[0]
    zero = jnp.zeros((shards, LANES), jnp.float32)
    tails = [zero, zero]
    for i in range(2 * owners):
        value = store[order[i]]
        for k in range(2):
            tails[k] = jnp.where(i >= 2 * g + k, jnp.maximum(tails[k], value), tails[k])
    lane = lax.broadcasted_iota(jnp.int32, (shards, LANES), 1)
    row = lax.broadcasted_iota(jnp.int32, (shards, LANES), 0)
    for k in range(2):
        moved = pltpu.roll(tails[k], LANES - 2 * width, 1)
        moved = pltpu.roll(moved, 0, 1, stride=width, stride_axis=0)
        out[k : k + 1, :] = jnp.sum(
            jnp.where(lane // width == row, moved, 0.0), axis=0, keepdims=True
        )
    part = lambda o: parts[pl.ds(pl.multiple_of(o * shards, shards), shards), :][:1]
    seen = part(g)
    left = pltpu.roll(part(jnp.maximum(g - 1, 0)), LANES - 2, 1)
    right = pltpu.roll(part(jnp.minimum(g + 1, owners - 1)), 2, 1)
    seen = jnp.maximum(seen, jnp.where(g > 0, left, 0.0))
    seen = jnp.maximum(seen, jnp.where(g < owners - 1, right, 0.0))
    observed[...] = seen[:, 98:100]


def call(kernel, outs, args, us, scratch=(), remote=()):
    scalar = [a.size <= 64 for a in args]
    many = isinstance(outs, list)
    made = pl.pallas_call(
        kernel,
        out_shape=tuple(outs) if many else outs,
        in_specs=[
            pl.BlockSpec(memory_space=pltpu.HBM) if i in remote else SM if k else VM
            for i, k in enumerate(scalar)
        ],
        out_specs=tuple([VM] * len(outs)) if many else VM,
        scratch_shapes=scratch,
        compiler_params=pltpu.CompilerParams(vmem_limit_bytes=24 << 20),
        cost_estimate=pl.CostEstimate(flops=int(us * 1e9), bytes_accessed=0, transcendentals=0),
    )
    args = [
        a
        if k
        else pltpu.with_memory_space_constraint(a, pltpu.HBM if i in remote else pltpu.VMEM)
        for i, (a, k) in enumerate(zip(args, scalar))
    ]
    return made(*args)


def shape(dims, kind=jnp.float32):
    return pltpu.VMEM(dims, kind)


def on_device(dosage, expression, perms, windows, order):
    variants, width = dosage.shape
    owners = lax.axis_size("gene")
    shards = 8
    samples = width * shards
    g, z, c = lax.axis_index("gene"), lax.axis_index("z"), lax.axis_index("core")
    place = jnp.stack([g, z, c]).astype(jnp.int32)
    packed, kept = call(
        pack_kernel,
        [shape((shards, 2, width + variants)), shape((variants, width), jnp.bfloat16)],
        [dosage, expression.T],
        2,
        [pltpu.VMEM((2, width), jnp.float32), pltpu.SemaphoreType.DMA((variants // LANES + 1,))],
        remote=(0, 1),
    )
    every = lax.all_to_all(packed, ("z", "core"), 0, 0, tiled=True)

    table_shape = shape((2, samples // LANES, TILE, LANES), jnp.bfloat16)
    first, table, stat = call(
        functools.partial(first_kernel, variants),
        [shape((9 * TILE, width), jnp.bfloat16), table_shape, shape((8, variants))],
        [place, windows, every, perms],
        9,
    )
    shuffled = [first]
    for h in range(1, CHUNKS):
        shuffled.append(
            call(
                functools.partial(later_kernel, h),
                shape((8 * TILE, width), jnp.bfloat16),
                [place, perms, table],
                9,
            )
        )
    ahead = [(i, (i + 1) % owners) for i in range(owners)]
    back = [(b, a) for a, b in ahead]
    halves = []
    for h, own in enumerate(shuffled):
        left = lax.ppermute(own, "gene", ahead)
        right = lax.ppermute(own, "gene", back)
        args = [left, own, right, kept, stat]
        if h == 0:
            outs = [shape((200, variants)), shape((8, LANES))]
            send, info = call(functools.partial(product_kernel, 1, True), outs, args, 1)
        else:
            send = call(
                functools.partial(product_kernel, 1, False), shape((192, variants)), args, 1
            )
        got = lax.ppermute(send, "core", [(0, 1), (1, 0)])
        keep = call(functools.partial(product_kernel, 0, False), shape((192, variants)), args, 1)
        halves += [keep, send, got] if h == 0 else [keep, got]
    own, *parts = call(
        split_kernel,
        [shape((104, variants))] + [shape((112, variants), jnp.int16)] * 3,
        halves,
        1,
        [pltpu.VMEM((3, 96, variants), jnp.float32)],
    )
    sums = []
    for k in range(1, 4):
        sums.append(lax.ppermute(parts[k - 1], "z", [(i, (i + k) % 4) for i in range(4)]))
    everyone = owners * shards
    lines = call(maxima_kernel, shape((everyone, LANES)), [place, info, stat, own, *sums], 2)
    lines = lax.all_to_all(
        lines.reshape(everyone, 1, LANES), ("gene", "z", "core"), 0, 0, tiled=True
    ).reshape(everyone, LANES)
    successive, observed = call(
        final_kernel,
        [jax.ShapeDtypeStruct((2, LANES), jnp.float32), jax.ShapeDtypeStruct((1, 2), jnp.float32)],
        [place, order, lines],
        2,
        [pltpu.VMEM((2 * owners, HALF, LANES), jnp.float32)],
    )
    return observed.reshape(2), successive


def solution(mesh):
    split = Mesh(mesh.devices.reshape(16, 4, 2), ("gene", "z", "core"))
    samp = ("z", "core")
    placed = (P("gene", samp), P(samp, "gene"), P(None, samp), P("gene", None), P())
    return jax.shard_map(
        on_device,
        mesh=split,
        in_specs=placed,
        out_specs=(P("gene"), P("gene", None)),
        check_vma=False,
    )
```

```python
import functools

import jax
import jax.numpy as jnp
from jax import lax
from jax.experimental import pallas as pl
from jax.experimental.pallas import tpu as pltpu
from jax.sharding import Mesh
from jax.sharding import PartitionSpec as P


epsilon = 1e-06
LANES = 128
TILE = 16
HALF = 8
CHUNKS = 2

VM = pl.BlockSpec(memory_space=pltpu.VMEM)
SM = pl.BlockSpec(memory_space=pltpu.SMEM)


def lane_gather(table, index):
    dims = lax.GatherDimensionNumbers(
        offset_dims=(),
        collapsed_slice_dims=(1,),
        start_index_map=(1,),
        operand_batching_dims=(0,),
        start_indices_batching_dims=(0,),
    )
    return lax.gather(
        table,
        index[..., None],
        dims,
        slice_sizes=(1, 1),
        mode=lax.GatherScatterMode.PROMISE_IN_BOUNDS,
    )


def gather_chunk(chunk, place, perms, table, out):
    z, c = place[1], place[2]
    table_rows = table.shape[1]
    tiles = perms.shape[1] // LANES
    group = 10

    def step(t, carry):
        block, part = t // (tiles // group), t % (tiles // group)
        kc, pair = block // 2, block % 2
        first = []
        for k in range(2):
            zz = lax.rem(z + pair * 2 + k, 4)
            cc = lax.rem(c + kc, 2)
            first.append(pl.multiple_of((zz * 2 + cc) * 2 * HALF + chunk * HALF, HALF))
        for u in range(group):
            lane = pl.ds(pl.multiple_of((part * group + u) * LANES, LANES), LANES)
            index = jnp.concatenate([perms[pl.ds(f, HALF), lane] for f in first], axis=0)
            low = (index & (LANES - 1)).astype(jnp.int16)
            high = (index >> 7).astype(jnp.int16)
            found = [jnp.zeros((TILE, LANES), jnp.bfloat16) for _ in range(2)]
            for r in range(table_rows):
                here = high == jnp.int16(r)
                for j in range(2):
                    found[j] = jnp.where(here, lane_gather(table[j, r], low), found[j])
            for j in range(2):
                row = pl.multiple_of(block * 2 * TILE + j * TILE, TILE)
                out[pl.ds(row, TILE), lane] = found[j]
        return carry

    lax.fori_loop(0, 4 * (tiles // group), step, 0)


def lane_sums(rows):
    return lax.dot_general(
        jnp.ones((8, LANES), jnp.float32),
        rows,
        (((1,), (1,)), ((), ())),
        precision=lax.Precision.HIGHEST,
        preferred_element_type=jnp.float32,
    )[:1]


def pack_kernel(dosage, expression, out, kept, levels, squares, done):
    shards, genes, _ = out.shape
    variants, width = dosage.shape
    pieces = variants // LANES
    copies = []
    for i in range(pieces):
        rows = pl.ds(i * LANES, LANES)
        copies.append(pltpu.make_async_copy(dosage.at[rows], kept.at[rows], done.at[i]))
        copies[-1].start()
    fetch = pltpu.make_async_copy(expression, levels, done.at[pieces])
    fetch.start()
    for i in range(pieces):
        copies[i].wait()
        square = jnp.zeros((LANES, LANES), jnp.float32)
        for k in range(width // LANES):
            v = kept[i * LANES : (i + 1) * LANES, k * LANES : (k + 1) * LANES].astype(jnp.float32)
            square = square + v * v
        squares[i * LANES : (i + 1) * LANES, :] = square
    moments = (times(jnp.ones((TILE, width), jnp.bfloat16), kept[...])[:1], lane_sums(squares[...]))
    fetch.wait()
    for d in range(shards):
        out[d, :, :width] = levels[...]
        for j in range(genes):
            out[d, j : j + 1, width:] = moments[j]


def first_kernel(variants, place, windows, every, perms, out, table, stat):
    z, c = place[1], place[2]
    shards, genes, wide = every.shape
    width = wide - variants
    samples = shards * width
    moments = jnp.sum(every[:, :, width:], axis=0)
    row_mean = moments[0:1] / samples
    spread = moments[1:2] / samples - row_mean * row_mean + epsilon
    stat[...] = jnp.zeros_like(stat)
    stat[0:1, :] = row_mean
    stat[1:2, :] = lax.rsqrt(spread * samples)
    own = every[z * 2 + c][:, :width]
    direct, sums = [], []
    for j in range(genes):
        x = every[:, j, :width]
        mean = jnp.sum(x, keepdims=True) / samples
        center = x - mean
        scale = lax.rsqrt(jnp.sum(center * center, keepdims=True) / samples + epsilon)
        scaled = (center * scale).astype(jnp.bfloat16).astype(jnp.float32)
        sums.append(jnp.sum(scaled, keepdims=True))
        for k in range(shards):
            for i in range(width // LANES):
                piece = scaled[k : k + 1, i * LANES : (i + 1) * LANES]
                table[j, k * (width // LANES) + i] = jnp.broadcast_to(piece, (TILE, LANES)).astype(
                    jnp.bfloat16
                )
        direct.append((own[j : j + 1] - mean) * scale)
    row = lax.broadcasted_iota(jnp.int32, (TILE, width), 0)
    lane = lax.broadcasted_iota(jnp.int32, (TILE, width), 1)
    extra = jnp.where(row == 0, direct[0], jnp.where(row == 1, direct[1], 0.0))
    for j in range(genes):
        for b in range(2):
            w = windows[j, b]
            digits = ((w >> 7).astype(jnp.float32), (w & 127).astype(jnp.float32))
            for d in range(2):
                extra = jnp.where((row == 2 + d) & (lane == j * 2 + b), digits[d], extra)
        rest = sums[j]
        for d in range(3):
            digit = rest.astype(jnp.bfloat16).astype(jnp.float32)
            rest = rest - digit
            extra = jnp.where((row == 4 + d) & (lane == j), digit, extra)
    out[8 * TILE : 9 * TILE, :] = extra.astype(jnp.bfloat16)
    gather_chunk(0, place, perms, table, out)


def later_kernel(chunk, place, perms, table, out):
    gather_chunk(chunk, place, perms, table, out)


def times(rows, dosage):
    return lax.dot_general(
        rows, dosage, (((1,), (1,)), ((), ())), preferred_element_type=jnp.float32
    )


def product_kernel(kc, with_direct, left, own, right, dosage, stat, *outs):
    blocks = [ref[kc * 4 * TILE : (kc + 1) * 4 * TILE, :] for ref in (left, own, right)]
    if with_direct:
        blocks += [ref[8 * TILE :, :] for ref in (left, own, right)]
    rows = jnp.concatenate(blocks, axis=0)
    mean, scale = stat[0:1, :], stat[1:2, :]
    got = (times(rows, dosage[...]) - jnp.sum(rows.astype(jnp.float32), axis=1, keepdims=True) * mean) * scale
    out = outs[0]
    for o in range(3):
        for kz in range(4):
            for j in range(2):
                src = o * 4 * TILE + (kz // 2) * 2 * TILE + j * TILE + (kz % 2) * HALF
                to = kz * 48 + (o * 2 + j) * HALF
                out[to : to + HALF, :] = got[src : src + HALF]
    if with_direct:
        first = 12 * TILE
        zero = jnp.zeros((2, got.shape[1]), jnp.float32)
        out[192:200, :] = jnp.concatenate(
            [got[first + o * TILE : first + o * TILE + 2] for o in range(3)] + [zero], axis=0
        )
        info = outs[1]
        info[...] = jnp.zeros_like(info)
        lane = lax.broadcasted_iota(jnp.int32, (1, LANES), 1)
        for o, ref in enumerate((left, own, right)):
            e = ref[8 * TILE :, :LANES].astype(jnp.float32)
            line = jnp.where(lane < 4, e[2:3] * 128.0 + e[3:4], 0.0)
            total = (e[4:5] + e[5:6]) + e[6:7]
            for j in range(2):
                line = jnp.where(lane == 4 + j, total[:, j : j + 1], line)
            info[o : o + 1, :] = line


LEVELS = 32767.0
PARTS = 256.0


def bound_code(largest):
    return jnp.clip(jnp.ceil(largest * PARTS), 1.0, LEVELS)


def coded(values, code):
    scaled = values * (LEVELS * PARTS / code)
    return jnp.clip(jnp.round(scaled), -LEVELS, LEVELS)


def to_int16(values):
    return values.astype(jnp.int32).astype(jnp.int16)


def split_kernel(*refs):
    *ins, own, m1, m2, m3, hold = refs
    keep, got = ins[0], ins[-1]
    variants = own.shape[1]
    largest = jnp.zeros((HALF, variants), jnp.float32)
    for kz in range(4):
        for t in range(6):
            at = kz * 48 + t * HALF
            v = keep[at : at + HALF, :] + got[at : at + HALF, :]
            if kz == 0:
                own[t * HALF : (t + 1) * HALF, :] = v
            else:
                hold[at - 48 : at - 40, :] = v
                largest = jnp.maximum(largest, jnp.abs(v))
    code = bound_code(jnp.max(largest, keepdims=True))
    if len(ins) == 3:
        direct = ins[1][192:200, :] + got[192:200, :]
        own[48:56, :] = direct
        direct_code = bound_code(jnp.max(jnp.abs(direct), keepdims=True))
        direct = to_int16(
            jnp.concatenate([coded(direct, direct_code), jnp.zeros_like(direct)], axis=0)
        )
        direct_code = to_int16(jnp.broadcast_to(direct_code, (TILE, LANES)))
    code_rows = to_int16(jnp.broadcast_to(code, (48, LANES)))
    for k, message in enumerate((m1, m2, m3)):
        for t in range(3):
            rows = hold[k * 48 + t * TILE : k * 48 + (t + 1) * TILE, :]
            message[t * TILE : (t + 1) * TILE, :variants] = to_int16(coded(rows, code))
        message[:48, variants:] = code_rows
        if len(ins) == 3:
            message[48:64, :variants] = direct
            message[48:64, variants:] = direct_code


def decoded(message, variants):
    q = message[...].astype(jnp.int32).astype(jnp.float32)
    return q[:, :variants] * (q[:, variants : variants + 1] * (1.0 / (LEVELS * PARTS)))


def maxima_kernel(place, info, stat, *refs):
    out = refs[-1]
    variants = stat.shape[1]
    chunks = []
    for h in range(CHUNKS):
        own, *messages = refs[4 * h : 4 * h + 4]
        rows = own.shape[0]
        total = own[...]
        for message in messages:
            total = total + decoded(message, variants)[:rows]
        chunks.append(total)
    direct = chunks[0][48:56]
    offset = stat[0:1, :] * stat[1:2, :]
    index = lax.broadcasted_iota(jnp.int32, (1, variants), 1) + place[0] * variants
    index = index.astype(jnp.float32)
    lane = lax.broadcasted_iota(jnp.int32, (HALF, LANES), 1)
    row = lax.broadcasted_iota(jnp.int32, (HALF, LANES), 0)
    tile = jnp.zeros((HALF, LANES), jnp.float32)
    seen = []
    for o in range(3):
        for j in range(2):
            n = o * 2 + j
            lo = info[o : o + 1, j * 2 : j * 2 + 1]
            hi = info[o : o + 1, j * 2 + 1 : j * 2 + 2]
            back = offset * info[o : o + 1, 4 + j : 5 + j]
            inside = (index >= lo) & (index < hi)
            for h in range(CHUNKS):
                v = jnp.abs(chunks[h][n * HALF : (n + 1) * HALF] + back)
                best = jnp.max(jnp.where(inside, v, 0.0), axis=1, keepdims=True)
                tile = jnp.where(lane // HALF == n * CHUNKS + h, best, tile)
            v = jnp.abs(direct[n : n + 1] + back)
            seen.append(jnp.max(jnp.where(inside, v, 0.0), axis=1, keepdims=True))
    line = jnp.sum(jnp.where(lane % HALF == row, tile, 0.0), axis=0, keepdims=True)
    for n in range(6):
        line = jnp.where(lane[:1] == 96 + n, seen[n], line)
    for i in range(out.shape[0] // HALF):
        out[i * HALF : (i + 1) * HALF, :] = jnp.broadcast_to(line, (HALF, LANES))


def final_kernel(place, order, parts, out, observed, store):
    shards = HALF
    owners = parts.shape[0] // shards
    block = lambda o: parts[o * shards : (o + 1) * shards, :]
    width = 2 * HALF
    for o in range(owners):
        best = block(o)
        if o > 0:
            best = jnp.maximum(best, pltpu.roll(block(o - 1), LANES - 2 * width, 1))
        if o < owners - 1:
            best = jnp.maximum(best, pltpu.roll(block(o + 1), 2 * width, 1))
        store[2 * o] = best
        store[2 * o + 1] = pltpu.roll(best, LANES - width, 1)
    g = place[0]
    zero = jnp.zeros((shards, LANES), jnp.float32)
    tails = [zero, zero]
    for i in range(2 * owners):
        value = store[order[i]]
        for k in range(2):
            tails[k] = jnp.where(i >= 2 * g + k, jnp.maximum(tails[k], value), tails[k])
    lane = lax.broadcasted_iota(jnp.int32, (shards, LANES), 1)
    row = lax.broadcasted_iota(jnp.int32, (shards, LANES), 0)
    for k in range(2):
        moved = pltpu.roll(tails[k], LANES - 2 * width, 1)
        moved = pltpu.roll(moved, 0, 1, stride=width, stride_axis=0)
        out[k : k + 1, :] = jnp.sum(
            jnp.where(lane // width == row, moved, 0.0), axis=0, keepdims=True
        )
    part = lambda o: parts[pl.ds(pl.multiple_of(o * shards, shards), shards), :][:1]
    seen = part(g)
    left = pltpu.roll(part(jnp.maximum(g - 1, 0)), LANES - 2, 1)
    right = pltpu.roll(part(jnp.minimum(g + 1, owners - 1)), 2, 1)
    seen = jnp.maximum(seen, jnp.where(g > 0, left, 0.0))
    seen = jnp.maximum(seen, jnp.where(g < owners - 1, right, 0.0))
    observed[...] = seen[:, 98:100]


def call(kernel, outs, args, us, scratch=(), remote=()):
    scalar = [a.size <= 64 for a in args]
    many = isinstance(outs, list)
    made = pl.pallas_call(
        kernel,
        out_shape=tuple(outs) if many else outs,
        in_specs=[
            pl.BlockSpec(memory_space=pltpu.HBM) if i in remote else SM if k else VM
            for i, k in enumerate(scalar)
        ],
        out_specs=tuple([VM] * len(outs)) if many else VM,
        scratch_shapes=scratch,
        compiler_params=pltpu.CompilerParams(vmem_limit_bytes=24 << 20),
        cost_estimate=pl.CostEstimate(flops=int(us * 1e9), bytes_accessed=0, transcendentals=0),
    )
    args = [
        a
        if k
        else pltpu.with_memory_space_constraint(a, pltpu.HBM if i in remote else pltpu.VMEM)
        for i, (a, k) in enumerate(zip(args, scalar))
    ]
    return made(*args)


def shape(dims, kind=jnp.float32):
    return pltpu.VMEM(dims, kind)


def on_device(dosage, expression, perms, windows, order):
    variants, width = dosage.shape
    owners = lax.axis_size("gene")
    shards = 8
    samples = width * shards
    g, z, c = lax.axis_index("gene"), lax.axis_index("z"), lax.axis_index("core")
    place = jnp.stack([g, z, c]).astype(jnp.int32)
    packed, kept = call(
        pack_kernel,
        [shape((shards, 2, width + variants)), shape((variants, width), jnp.bfloat16)],
        [dosage, expression.T],
        2,
        [
            pltpu.VMEM((2, width), jnp.float32),
            pltpu.VMEM((variants, LANES), jnp.float32),
            pltpu.SemaphoreType.DMA((variants // LANES + 1,)),
        ],
        remote=(0, 1),
    )
    every = lax.all_to_all(packed, ("z", "core"), 0, 0, tiled=True)

    table_shape = shape((2, samples // LANES, TILE, LANES), jnp.bfloat16)
    first, table, stat = call(
        functools.partial(first_kernel, variants),
        [shape((9 * TILE, width), jnp.bfloat16), table_shape, shape((8, variants))],
        [place, windows, every, perms],
        9,
    )
    shuffled = [first]
    for h in range(1, CHUNKS):
        shuffled.append(
            call(
                functools.partial(later_kernel, h),
                shape((8 * TILE, width), jnp.bfloat16),
                [place, perms, table],
                9,
            )
        )
    ahead = [(i, (i + 1) % owners) for i in range(owners)]
    back = [(b, a) for a, b in ahead]
    sums = []
    for h, own in enumerate(shuffled):
        left = lax.ppermute(own, "gene", ahead)
        right = lax.ppermute(own, "gene", back)
        args = [left, own, right, kept, stat]
        if h == 0:
            outs = [shape((200, variants)), shape((8, LANES))]
            send, info = call(functools.partial(product_kernel, 1, True), outs, args, 1)
        else:
            send = call(
                functools.partial(product_kernel, 1, False), shape((192, variants)), args, 1
            )
        got = lax.ppermute(send, "core", [(0, 1), (1, 0)])
        keep = call(functools.partial(product_kernel, 0, False), shape((192, variants)), args, 1)
        depth = 56 if h == 0 else 48
        own, *parts = call(
            split_kernel,
            [shape((depth, variants))]
            + [shape((64 if h == 0 else 48, variants + LANES), jnp.int16)] * 3,
            [keep, send, got] if h == 0 else [keep, got],
            1,
            [pltpu.VMEM((144, variants), jnp.float32)],
        )
        sums.append(own)
        for k in range(1, 4):
            sums.append(lax.ppermute(parts[k - 1], "z", [(i, (i + k) % 4) for i in range(4)]))
    everyone = owners * shards
    lines = call(maxima_kernel, shape((everyone, LANES)), [place, info, stat, *sums], 2)
    lines = lax.all_to_all(
        lines.reshape(everyone, 1, LANES), ("gene", "z", "core"), 0, 0, tiled=True
    ).reshape(everyone, LANES)
    successive, observed = call(
        final_kernel,
        [jax.ShapeDtypeStruct((2, LANES), jnp.float32), jax.ShapeDtypeStruct((1, 2), jnp.float32)],
        [place, order, lines],
        2,
        [pltpu.VMEM((2 * owners, HALF, LANES), jnp.float32)],
    )
    return observed.reshape(2), successive


def solution(mesh):
    split = Mesh(mesh.devices.reshape(16, 4, 2), ("gene", "z", "core"))
    samp = ("z", "core")
    placed = (P("gene", samp), P(samp, "gene"), P(None, samp), P("gene", None), P())
    return jax.shard_map(
        on_device,
        mesh=split,
        in_specs=placed,
        out_specs=(P("gene"), P("gene", None)),
        check_vma=False,
    )
```

```python
import functools

import jax
import jax.numpy as jnp
from jax import lax
from jax.experimental import pallas as pl
from jax.experimental.pallas import tpu as pltpu
from jax.sharding import Mesh
from jax.sharding import PartitionSpec as P


epsilon = 1e-06
LANES = 128
TILE = 16
HALF = 8
CHUNKS = 2

VM = pl.BlockSpec(memory_space=pltpu.VMEM)
SM = pl.BlockSpec(memory_space=pltpu.SMEM)


def lane_gather(table, index):
    dims = lax.GatherDimensionNumbers(
        offset_dims=(),
        collapsed_slice_dims=(1,),
        start_index_map=(1,),
        operand_batching_dims=(0,),
        start_indices_batching_dims=(0,),
    )
    return lax.gather(
        table,
        index[..., None],
        dims,
        slice_sizes=(1, 1),
        mode=lax.GatherScatterMode.PROMISE_IN_BOUNDS,
    )


def look_up(chunk, genes, place, perms, theirs, table, out):
    z, c = place[1], place[2]
    table_rows = table.shape[1]
    width = perms.shape[1]

    def step(pair, carry):
        first = []
        for k in range(2):
            d = lax.rem(z + pair * 2 + k, 4) * 2 + c
            first.append(pl.multiple_of(d * 2 * HALF + chunk * HALF, HALF))
        for u in range(2 * width // LANES):
            source = perms if u < width // LANES else theirs
            lane = u % (width // LANES) * LANES
            rows = [source[pl.ds(f, HALF), lane : lane + LANES] for f in first]
            index = jnp.concatenate(rows, axis=0)
            low = (index & (LANES - 1)).astype(jnp.int16)
            high = (index >> 7).astype(jnp.int16)
            found = [jnp.zeros((TILE, LANES), jnp.bfloat16) for _ in genes]
            for r in range(table_rows):
                here = high == jnp.int16(r)
                for n, j in enumerate(genes):
                    found[n] = jnp.where(here, lane_gather(table[j, r], low), found[n])
            for n in range(len(genes)):
                row = pl.multiple_of(n * 2 * TILE + pair * TILE, TILE)
                out[pl.ds(row, TILE), u * LANES : (u + 1) * LANES] = found[n]
        return carry

    lax.fori_loop(0, 2, step, 0)


def lane_sums(rows):
    return lax.dot_general(
        jnp.ones((8, LANES), jnp.float32),
        rows,
        (((1,), (1,)), ((), ())),
        precision=lax.Precision.HIGHEST,
        preferred_element_type=jnp.float32,
    )[:1]


def pack_kernel(dosage, expression, out, kept, levels, sums, done):
    shards, genes, _ = out.shape
    variants, width = dosage.shape
    pieces = variants // LANES
    copies = []
    for i in range(pieces):
        rows = pl.ds(i * LANES, LANES)
        copies.append(pltpu.make_async_copy(dosage.at[rows], kept.at[rows], done.at[i]))
        copies[-1].start()
    fetch = pltpu.make_async_copy(expression, levels, done.at[pieces])
    fetch.start()
    for i in range(pieces):
        copies[i].wait()
        rows = slice(i * LANES, (i + 1) * LANES)
        total = jnp.zeros((LANES, LANES), jnp.float32)
        square = jnp.zeros((LANES, LANES), jnp.float32)
        for k in range(width // LANES):
            v = kept[rows, k * LANES : (k + 1) * LANES].astype(jnp.float32)
            total = total + v
            square = square + v * v
        sums[0, rows, :] = total
        sums[1, rows, :] = square
    moments = [lane_sums(sums[j]) for j in range(2)]
    fetch.wait()
    for d in range(shards):
        out[d, :, :width] = levels[...]
        for j in range(genes):
            out[d, j : j + 1, width:] = moments[j]


def first_kernel(variants, place, windows, every, perms, theirs, out, table, stat):
    z, c = place[1], place[2]
    shards, genes, wide = every.shape
    width = wide - variants
    samples = shards * width
    moments = jnp.sum(every[:, :, width:], axis=0)
    row_mean = moments[0:1] / samples
    spread = moments[1:2] / samples - row_mean * row_mean + epsilon
    stat[...] = jnp.zeros_like(stat)
    stat[0:1, :] = row_mean
    stat[1:2, :] = lax.rsqrt(spread * samples)
    own = jnp.concatenate([every[z * 2 + c][:, :width], every[z * 2 + 1 - c][:, :width]], axis=1)
    direct, sums = [], []
    for j in range(genes):
        x = every[:, j, :width]
        mean = jnp.sum(x, keepdims=True) / samples
        center = x - mean
        scale = lax.rsqrt(jnp.sum(center * center, keepdims=True) / samples + epsilon)
        scaled = (center * scale).astype(jnp.bfloat16).astype(jnp.float32)
        sums.append(jnp.sum(scaled, keepdims=True))
        for k in range(shards):
            for i in range(width // LANES):
                piece = scaled[k : k + 1, i * LANES : (i + 1) * LANES]
                table[j, k * (width // LANES) + i] = jnp.broadcast_to(piece, (TILE, LANES)).astype(
                    jnp.bfloat16
                )
        direct.append((own[j : j + 1] - mean) * scale)
    row = lax.broadcasted_iota(jnp.int32, (TILE, 2 * width), 0)
    lane = lax.broadcasted_iota(jnp.int32, (TILE, 2 * width), 1)
    extra = jnp.where(row == 0, direct[0], jnp.where(row == 1, direct[1], 0.0))
    for j in range(genes):
        for b in range(2):
            w = windows[j, b]
            digits = ((w >> 7).astype(jnp.float32), (w & 127).astype(jnp.float32))
            for d in range(2):
                extra = jnp.where((row == 2 + d) & (lane == j * 2 + b), digits[d], extra)
        rest = sums[j]
        for d in range(3):
            digit = rest.astype(jnp.bfloat16).astype(jnp.float32)
            rest = rest - digit
            extra = jnp.where((row == 4 + d) & (lane == j), digit, extra)
    out[4 * TILE : 5 * TILE, :] = extra.astype(jnp.bfloat16)
    look_up(0, (0, 1), place, perms, theirs, table, out)


def later_kernel(gene, place, perms, theirs, table, out):
    look_up(1, (gene,), place, perms, theirs, table, out)


def times(rows, dosage):
    return lax.dot_general(
        rows, dosage, (((1,), (1,)), ((), ())), preferred_element_type=jnp.float32
    )


LEVELS = 32767.0
PARTS = 256.0


def bound_code(largest):
    return jnp.clip(jnp.ceil(largest * PARTS), 1.0, LEVELS)


def coded(values, code):
    scaled = values * (LEVELS * PARTS / code)
    return jnp.clip(jnp.round(scaled), -LEVELS, LEVELS)


def to_int16(values):
    return values.astype(jnp.int32).astype(jnp.int16)


def sums_kernel(chunk, *refs):
    count = 3 if chunk == 0 else 6
    blocks = refs[:count]
    kept, theirs, stat, own, m1, m2, m3 = refs[count : count + 7]
    variants, width = kept.shape
    pieces = []
    for o in range(3):
        for j in range(2):
            if chunk == 0:
                pieces.append(blocks[o][j * 2 * TILE : (j + 1) * 2 * TILE, :])
            else:
                pieces.append(blocks[j * 3 + o][...])
    if chunk == 0:
        pieces += [block[4 * TILE :, :] for block in blocks]
    rows = jnp.concatenate(pieces, axis=0)
    both = times(rows[:, :width], kept[...]) + times(rows[:, width:], theirs[...])
    column = jnp.sum(rows.astype(jnp.float32), axis=1, keepdims=True)
    got = (both - column * stat[0:1, :]) * stat[1:2, :]
    part = lambda n, kz: got[n * 2 * TILE + kz * HALF : n * 2 * TILE + (kz + 1) * HALF]
    for n in range(6):
        own[n * HALF : (n + 1) * HALF, :] = part(n, 0)
    largest = jnp.abs(part(0, 1))
    for n in range(6):
        for kz in range(1, 4):
            largest = jnp.maximum(largest, jnp.abs(part(n, kz)))
    code = bound_code(jnp.max(largest, keepdims=True))
    code_rows = to_int16(jnp.broadcast_to(code, (48, LANES)))
    for k, message in enumerate((m1, m2, m3)):
        for t in range(3):
            values = jnp.concatenate([part(2 * t, k + 1), part(2 * t + 1, k + 1)], axis=0)
            message[t * TILE : (t + 1) * TILE, :variants] = to_int16(coded(values, code))
        message[:48, variants:] = code_rows
    if chunk == 0:
        first = 12 * TILE
        zero = jnp.zeros((2, variants), jnp.float32)
        direct = jnp.concatenate(
            [got[first + o * TILE : first + o * TILE + 2] for o in range(3)] + [zero], axis=0
        )
        own[48:56, :] = direct
        code = bound_code(jnp.max(jnp.abs(direct), keepdims=True))
        tail = to_int16(jnp.concatenate([coded(direct, code), jnp.zeros_like(direct)], axis=0))
        code = to_int16(jnp.broadcast_to(code, (TILE, LANES)))
        for message in (m1, m2, m3):
            message[48:64, :variants] = tail
            message[48:64, variants:] = code
        info = refs[-1]
        info[...] = jnp.zeros_like(info)
        lane = lax.broadcasted_iota(jnp.int32, (1, LANES), 1)
        for o, block in enumerate(blocks):
            e = block[4 * TILE :, :LANES].astype(jnp.float32)
            line = jnp.where(lane < 4, e[2:3] * 128.0 + e[3:4], 0.0)
            total = (e[4:5] + e[5:6]) + e[6:7]
            for j in range(2):
                line = jnp.where(lane == 4 + j, total[:, j : j + 1], line)
            info[o : o + 1, :] = line


def decoded(message, variants):
    q = message[...].astype(jnp.int32).astype(jnp.float32)
    return q[:, :variants] * (q[:, variants : variants + 1] * (1.0 / (LEVELS * PARTS)))


def maxima_kernel(place, info, stat, *refs):
    out = refs[-1]
    variants = stat.shape[1]
    chunks = []
    for h in range(CHUNKS):
        own, *messages = refs[4 * h : 4 * h + 4]
        rows = own.shape[0]
        total = own[...]
        for message in messages:
            total = total + decoded(message, variants)[:rows]
        chunks.append(total)
    direct = chunks[0][48:56]
    offset = stat[0:1, :] * stat[1:2, :]
    index = lax.broadcasted_iota(jnp.int32, (1, variants), 1) + place[0] * variants
    index = index.astype(jnp.float32)
    lane = lax.broadcasted_iota(jnp.int32, (HALF, LANES), 1)
    row = lax.broadcasted_iota(jnp.int32, (HALF, LANES), 0)
    tile = jnp.zeros((HALF, LANES), jnp.float32)
    seen = []
    for o in range(3):
        for j in range(2):
            n = o * 2 + j
            lo = info[o : o + 1, j * 2 : j * 2 + 1]
            hi = info[o : o + 1, j * 2 + 1 : j * 2 + 2]
            back = offset * info[o : o + 1, 4 + j : 5 + j]
            inside = (index >= lo) & (index < hi)
            for h in range(CHUNKS):
                v = jnp.abs(chunks[h][n * HALF : (n + 1) * HALF] + back)
                best = jnp.max(jnp.where(inside, v, 0.0), axis=1, keepdims=True)
                tile = jnp.where(lane // HALF == n * CHUNKS + h, best, tile)
            v = jnp.abs(direct[n : n + 1] + back)
            seen.append(jnp.max(jnp.where(inside, v, 0.0), axis=1, keepdims=True))
    line = jnp.sum(jnp.where(lane % HALF == row, tile, 0.0), axis=0, keepdims=True)
    for n in range(6):
        line = jnp.where(lane[:1] == 96 + n, seen[n], line)
    for i in range(out.shape[0] // HALF):
        out[i * HALF : (i + 1) * HALF, :] = jnp.broadcast_to(line, (HALF, LANES))


def final_kernel(place, order, parts, out, observed, store):
    shards = HALF
    owners = parts.shape[0] // shards
    block = lambda o: parts[o * shards : (o + 1) * shards, :]
    width = 2 * HALF
    for o in range(owners):
        best = block(o)
        if o > 0:
            best = jnp.maximum(best, pltpu.roll(block(o - 1), LANES - 2 * width, 1))
        if o < owners - 1:
            best = jnp.maximum(best, pltpu.roll(block(o + 1), 2 * width, 1))
        store[2 * o] = best
        store[2 * o + 1] = pltpu.roll(best, LANES - width, 1)
    g = place[0]
    zero = jnp.zeros((shards, LANES), jnp.float32)
    tails = [zero, zero]
    for i in range(2 * owners):
        value = store[order[i]]
        for k in range(2):
            tails[k] = jnp.where(i >= 2 * g + k, jnp.maximum(tails[k], value), tails[k])
    lane = lax.broadcasted_iota(jnp.int32, (shards, LANES), 1)
    row = lax.broadcasted_iota(jnp.int32, (shards, LANES), 0)
    for k in range(2):
        moved = pltpu.roll(tails[k], LANES - 2 * width, 1)
        moved = pltpu.roll(moved, 0, 1, stride=width, stride_axis=0)
        out[k : k + 1, :] = jnp.sum(
            jnp.where(lane // width == row, moved, 0.0), axis=0, keepdims=True
        )
    part = lambda o: parts[pl.ds(pl.multiple_of(o * shards, shards), shards), :][:1]
    seen = part(g)
    left = pltpu.roll(part(jnp.maximum(g - 1, 0)), LANES - 2, 1)
    right = pltpu.roll(part(jnp.minimum(g + 1, owners - 1)), 2, 1)
    seen = jnp.maximum(seen, jnp.where(g > 0, left, 0.0))
    seen = jnp.maximum(seen, jnp.where(g < owners - 1, right, 0.0))
    observed[...] = seen[:, 98:100]


def call(kernel, outs, args, us, scratch=(), remote=()):
    scalar = [a.size <= 64 for a in args]
    many = isinstance(outs, list)
    made = pl.pallas_call(
        kernel,
        out_shape=tuple(outs) if many else outs,
        in_specs=[
            pl.BlockSpec(memory_space=pltpu.HBM) if i in remote else SM if k else VM
            for i, k in enumerate(scalar)
        ],
        out_specs=tuple([VM] * len(outs)) if many else VM,
        scratch_shapes=scratch,
        compiler_params=pltpu.CompilerParams(vmem_limit_bytes=24 << 20),
        cost_estimate=pl.CostEstimate(flops=int(us * 1e9), bytes_accessed=0, transcendentals=0),
    )
    args = [
        a
        if k
        else pltpu.with_memory_space_constraint(a, pltpu.HBM if i in remote else pltpu.VMEM)
        for i, (a, k) in enumerate(zip(args, scalar))
    ]
    return made(*args)


def shape(dims, kind=jnp.float32):
    return pltpu.VMEM(dims, kind)


def on_device(dosage, expression, perms, windows, order):
    variants, width = dosage.shape
    owners = lax.axis_size("gene")
    shards = 8
    samples = width * shards
    g, z, c = lax.axis_index("gene"), lax.axis_index("z"), lax.axis_index("core")
    place = jnp.stack([g, z, c]).astype(jnp.int32)
    mates = [(0, 1), (1, 0)]
    their_perms = lax.ppermute(perms, "core", mates)
    theirs = lax.ppermute(dosage, "core", mates)
    packed = call(
        pack_kernel,
        shape((shards, 2, width + variants)),
        [dosage, expression.T],
        2,
        [
            pltpu.VMEM((variants, width), jnp.bfloat16),
            pltpu.VMEM((2, width), jnp.float32),
            pltpu.VMEM((2, variants, LANES), jnp.float32),
            pltpu.SemaphoreType.DMA((variants // LANES + 1,)),
        ],
        remote=(0, 1),
    )
    every = lax.all_to_all(packed, ("z", "core"), 0, 0, tiled=True)

    table_shape = shape((2, samples // LANES, TILE, LANES), jnp.bfloat16)
    first, table, stat = call(
        functools.partial(first_kernel, variants),
        [shape((5 * TILE, 2 * width), jnp.bfloat16), table_shape, shape((8, variants))],
        [place, windows, every, perms, their_perms],
        9,
    )
    shuffled = [first]
    for j in range(2):
        shuffled.append(
            call(
                functools.partial(later_kernel, j),
                shape((2 * TILE, 2 * width), jnp.bfloat16),
                [place, perms, their_perms, table],
                4,
            )
        )
    ahead = [(i, (i + 1) % owners) for i in range(owners)]
    back = [(b, a) for a, b in ahead]
    around = []
    for own in shuffled:
        left = lax.ppermute(own, "gene", ahead)
        right = lax.ppermute(own, "gene", back)
        around.append([left, own, right])
    sums = []
    for h in range(CHUNKS):
        depth, deep = (56, 64) if h == 0 else (48, 48)
        outs = [shape((depth, variants))] + [shape((deep, variants + LANES), jnp.int16)] * 3
        own, *parts = call(
            functools.partial(sums_kernel, h),
            outs + ([shape((8, LANES))] if h == 0 else []),
            (around[0] if h == 0 else around[1] + around[2]) + [dosage, theirs, stat],
            2,
        )
        if h == 0:
            info = parts.pop()
        sums.append(own)
        for k in range(1, 4):
            sums.append(lax.ppermute(parts[k - 1], "z", [(i, (i + k) % 4) for i in range(4)]))
    everyone = owners * shards
    lines = call(maxima_kernel, shape((everyone, LANES)), [place, info, stat, *sums], 2)
    lines = lax.all_to_all(
        lines.reshape(everyone, 1, LANES), ("gene", "z", "core"), 0, 0, tiled=True
    ).reshape(everyone, LANES)
    successive, observed = call(
        final_kernel,
        [jax.ShapeDtypeStruct((2, LANES), jnp.float32), jax.ShapeDtypeStruct((1, 2), jnp.float32)],
        [place, order, lines],
        2,
        [pltpu.VMEM((2 * owners, HALF, LANES), jnp.float32)],
    )
    return observed.reshape(2), successive


def solution(mesh):
    split = Mesh(mesh.devices.reshape(16, 4, 2), ("gene", "z", "core"))
    samp = ("z", "core")
    placed = (P("gene", samp), P(samp, "gene"), P(None, samp), P("gene", None), P())
    return jax.shard_map(
        on_device,
        mesh=split,
        in_specs=placed,
        out_specs=(P("gene"), P("gene", None)),
        check_vma=False,
    )
```

```python
import functools

import jax
import jax.numpy as jnp
from jax import lax
from jax.experimental import pallas as pl
from jax.experimental.pallas import tpu as pltpu
from jax.sharding import Mesh
from jax.sharding import PartitionSpec as P


epsilon = 1e-06
LANES = 128
TILE = 16
HALF = 8
CHUNKS = 2

VM = pl.BlockSpec(memory_space=pltpu.VMEM)
SM = pl.BlockSpec(memory_space=pltpu.SMEM)


def lane_gather(table, index):
    dims = lax.GatherDimensionNumbers(
        offset_dims=(),
        collapsed_slice_dims=(1,),
        start_index_map=(1,),
        operand_batching_dims=(0,),
        start_indices_batching_dims=(0,),
    )
    return lax.gather(
        table,
        index[..., None],
        dims,
        slice_sizes=(1, 1),
        mode=lax.GatherScatterMode.PROMISE_IN_BOUNDS,
    )


def look_up(chunk, genes, place, perms, theirs, table, out):
    z, c = place[1], place[2]
    table_rows = table.shape[1]
    width = perms.shape[1]

    def step(pair, carry):
        first = []
        for k in range(2):
            d = lax.rem(z + pair * 2 + k, 4) * 2 + c
            first.append(pl.multiple_of(d * 2 * HALF + chunk * HALF, HALF))
        for u in range(2 * width // LANES):
            source = perms if u < width // LANES else theirs
            lane = u % (width // LANES) * LANES
            rows = [source[pl.ds(f, HALF), lane : lane + LANES] for f in first]
            index = jnp.concatenate(rows, axis=0)
            low = (index & (LANES - 1)).astype(jnp.int16)
            high = (index >> 7).astype(jnp.int16)
            found = [jnp.zeros((TILE, LANES), jnp.bfloat16) for _ in genes]
            for r in range(table_rows):
                here = high == jnp.int16(r)
                for n, j in enumerate(genes):
                    found[n] = jnp.where(here, lane_gather(table[j, r], low), found[n])
            for n in range(len(genes)):
                row = pl.multiple_of(n * 2 * TILE + pair * TILE, TILE)
                out[pl.ds(row, TILE), u * LANES : (u + 1) * LANES] = found[n]
        return carry

    lax.fori_loop(0, 2, step, 0)


def lane_sums(rows):
    return lax.dot_general(
        jnp.ones((8, LANES), jnp.float32),
        rows,
        (((1,), (1,)), ((), ())),
        precision=lax.Precision.HIGHEST,
        preferred_element_type=jnp.float32,
    )[:1]


def copies_kernel(expression, out, done):
    copies = [
        pltpu.make_async_copy(expression, out.at[d], done.at[d]) for d in range(out.shape[0])
    ]
    for copy in copies:
        copy.start()
    for copy in copies:
        copy.wait()


def moments_kernel(dosage, theirs, out, sums):
    variants, width = dosage.shape

    def step(i, carry):
        rows = pl.ds(pl.multiple_of(i * LANES, LANES), LANES)
        total = jnp.zeros((LANES, LANES), jnp.float32)
        square = jnp.zeros((LANES, LANES), jnp.float32)
        for source in (dosage, theirs):
            for k in range(width // LANES):
                v = source[rows, k * LANES : (k + 1) * LANES].astype(jnp.float32)
                total = total + v
                square = square + v * v
        sums[0, rows, :] = total
        sums[1, rows, :] = square
        return carry

    lax.fori_loop(0, variants // LANES, step, 0)
    out[...] = jnp.zeros_like(out)
    for j in range(2):
        out[j : j + 1, :] = lane_sums(sums[j])


def first_kernel(place, windows, every, perms, theirs, out, table):
    z, c = place[1], place[2]
    shards, genes, width = every.shape
    samples = shards * width
    own = jnp.concatenate([every[z * 2 + c], every[z * 2 + 1 - c]], axis=1)
    direct = []
    for j in range(genes):
        x = every[:, j, :]
        mean = jnp.sum(x, keepdims=True) / samples
        center = x - mean
        scale = lax.rsqrt(jnp.sum(center * center, keepdims=True) / samples + epsilon)
        scaled = center * scale
        for k in range(shards):
            for i in range(width // LANES):
                piece = scaled[k : k + 1, i * LANES : (i + 1) * LANES]
                table[j, k * (width // LANES) + i] = jnp.broadcast_to(piece, (TILE, LANES)).astype(
                    jnp.bfloat16
                )
        direct.append((own[j : j + 1] - mean) * scale)
    row = lax.broadcasted_iota(jnp.int32, (TILE, 2 * width), 0)
    lane = lax.broadcasted_iota(jnp.int32, (TILE, 2 * width), 1)
    extra = jnp.where(row == 0, direct[0], jnp.where(row == 1, direct[1], 0.0))
    for j in range(genes):
        for b in range(2):
            w = windows[j, b]
            digits = ((w >> 7).astype(jnp.float32), (w & 127).astype(jnp.float32))
            for d in range(2):
                extra = jnp.where((row == 2 + d) & (lane == j * 2 + b), digits[d], extra)
    out[4 * TILE : 5 * TILE, :] = extra.astype(jnp.bfloat16)
    look_up(0, (0, 1), place, perms, theirs, table, out)


def later_kernel(chunk, place, perms, theirs, table, out):
    look_up(chunk, (0, 1), place, perms, theirs, table, out)


def times(rows, dosage):
    return lax.dot_general(
        rows, dosage, (((1,), (1,)), ((), ())), preferred_element_type=jnp.float32
    )


LEVELS = 32767.0
PARTS = 256.0


def bound_code(largest):
    return jnp.clip(jnp.ceil(largest * PARTS), 1.0, LEVELS)


def coded(values, code):
    scaled = values * (LEVELS * PARTS / code)
    return jnp.clip(jnp.round(scaled), -LEVELS, LEVELS)


def to_int16(values):
    return values.astype(jnp.int32).astype(jnp.int16)


def digits(x):
    whole = jnp.floor(x)
    rest = (x - whole) * 32768.0
    high = jnp.floor(rest)
    return whole, high, jnp.floor((rest - high) * 32768.0)


def undigits(whole, high, low):
    return whole + (high + low * (1.0 / 32768.0)) * (1.0 / 32768.0)


def mean_and_size(total, square, count):
    mean = total / count
    return mean, jnp.sqrt(jnp.maximum(square - total * mean, 0.0) + count * epsilon)


def sums_kernel(chunk, *refs):
    blocks = refs[:3]
    dosage, theirs, stat, own, m1, m2, m3 = refs[3:10]
    variants, width = dosage.shape
    rows = jnp.concatenate([block[: 4 * TILE, :] for block in blocks], axis=0)
    if chunk == 0:
        rows = jnp.concatenate([rows] + [block[4 * TILE :, :] for block in blocks], axis=0)
    both = times(rows[:, :width], dosage[...]) + times(rows[:, width:], theirs[...])
    column = jnp.sum(rows.astype(jnp.float32), axis=1, keepdims=True)
    mean, size = mean_and_size(stat[0:1, :], stat[1:2, :], 2.0 * width)
    got = (both - column * mean) * (1.0 / size)
    column = jnp.broadcast_to(column, (column.shape[0], LANES))
    at = lambda n, kz: slice(n * 2 * TILE + kz * HALF, n * 2 * TILE + (kz + 1) * HALF)
    for n in range(6):
        own[n * HALF : (n + 1) * HALF, :] = both[at(n, 0)]
    largest = jnp.abs(got[at(0, 1)])
    for n in range(6):
        for kz in range(1, 4):
            largest = jnp.maximum(largest, jnp.abs(got[at(n, kz)]))

    def beside(code, columns):
        lane = lax.broadcasted_iota(jnp.int32, columns.shape, 1)
        whole, high, low = digits(columns)
        line = jnp.where(lane == 1, whole, jnp.where(lane == 2, high, low))
        return to_int16(jnp.where(lane == 0, code, line))

    code = bound_code(jnp.max(largest, keepdims=True))
    for k, message in enumerate((m1, m2, m3)):
        for t in range(3):
            pair = [at(2 * t, k + 1), at(2 * t + 1, k + 1)]
            values = jnp.concatenate([got[p] for p in pair], axis=0)
            columns = jnp.concatenate([column[p] for p in pair], axis=0)
            message[t * TILE : (t + 1) * TILE, :variants] = to_int16(coded(values, code))
            message[t * TILE : (t + 1) * TILE, variants:] = beside(code, columns)
    if chunk == 0:
        spots = [slice((12 + o) * TILE, (12 + o) * TILE + 2) for o in range(3)]
        gather = lambda x: jnp.concatenate([x[p] for p in spots] + [jnp.zeros_like(x[:2])], axis=0)
        own[48:56, :] = gather(both)
        values, columns = gather(got), gather(column)
        code = bound_code(jnp.max(jnp.abs(values), keepdims=True))
        rest = list(digits(stat[0:1, :]) + digits(stat[1:2, :]))
        rest.append(jnp.zeros((2, variants), jnp.float32))
        tail = to_int16(jnp.concatenate([coded(values, code)] + rest, axis=0))
        side = beside(code, jnp.concatenate([columns, jnp.zeros_like(columns)], axis=0))
        for message in (m1, m2, m3):
            message[48:64, :variants] = tail
            message[48:64, variants:] = side
        info = refs[-1]
        info[...] = jnp.zeros_like(info)
        for o, block in enumerate(blocks):
            e = block[4 * TILE :, :LANES].astype(jnp.float32)
            info[o : o + 1, :] = e[2:3] * 128.0 + e[3:4]


def added(own, messages, means, sizes):
    total = own[...]
    rows, variants = total.shape
    for message, mean, size in zip(messages, means, sizes):
        side = message[:rows, variants:].astype(jnp.int32).astype(jnp.float32)
        column = undigits(side[:, 1:2], side[:, 2:3], side[:, 3:4])
        unit = side[:, 0:1] * (1.0 / (LEVELS * PARTS))
        codes = message[:rows, :variants].astype(jnp.int32).astype(jnp.float32)
        total = total + (codes * unit * size + column * mean)
    return total


def inside_rows(place, info, variants):
    index = lax.broadcasted_iota(jnp.int32, (1, variants), 1) + place[0] * variants
    index = index.astype(jnp.float32)
    for o in range(3):
        for j in range(2):
            lo = info[o : o + 1, j * 2 : j * 2 + 1]
            hi = info[o : o + 1, j * 2 + 1 : j * 2 + 2]
            yield (index >= lo) & (index < hi)


def best_tile(tile, h, total, inside):
    lane = lax.broadcasted_iota(jnp.int32, (HALF, LANES), 1)
    for n, mask in enumerate(inside):
        v = jnp.abs(total[n * HALF : (n + 1) * HALF])
        best = jnp.max(jnp.where(mask, v, 0.0), axis=1, keepdims=True)
        tile = jnp.where(lane // HALF == n * CHUNKS + h, best, tile)
    return tile


def early_kernel(samples, place, info, stat, own, m1, m2, m3, out, aux):
    variants = own.shape[1]
    count = samples / 4.0
    total, square = stat[0:1, :], stat[1:2, :]
    means, sizes = [], []
    for message in (m1, m2, m3):
        d = message[48:64, :variants].astype(jnp.int32).astype(jnp.float32)
        their_total = undigits(d[8:9], d[9:10], d[10:11])
        their_square = undigits(d[11:12], d[12:13], d[13:14])
        mean, size = mean_and_size(their_total, their_square, count)
        means.append(mean)
        sizes.append(size)
        total = total + their_total
        square = square + their_square
    row_mean = total / samples
    spread = square / samples - row_mean * row_mean + epsilon
    scale = lax.rsqrt(spread * samples)
    aux[0:1, :] = scale
    for q in range(3):
        aux[1 + q : 2 + q, :] = means[q]
        aux[4 + q : 5 + q, :] = sizes[q]
    aux[7:8, :] = jnp.zeros_like(scale)
    sums = added(own, (m1, m2, m3), means, sizes) * scale
    inside = list(inside_rows(place, info, variants))
    tile = best_tile(jnp.zeros((HALF, LANES), jnp.float32), 0, sums, inside)
    lane = lax.broadcasted_iota(jnp.int32, (HALF, LANES), 1)
    for n, mask in enumerate(inside):
        v = jnp.abs(sums[48 + n : 49 + n])
        best = jnp.max(jnp.where(mask, v, 0.0), axis=1, keepdims=True)
        tile = jnp.where(lane == 96 + n, best, tile)
    out[...] = tile


def maxima_kernel(place, info, aux, tile, own, m1, m2, m3, out):
    variants = own.shape[1]
    means = [aux[1 + q : 2 + q, :] for q in range(3)]
    sizes = [aux[4 + q : 5 + q, :] for q in range(3)]
    sums = added(own, (m1, m2, m3), means, sizes) * aux[0:1, :]
    tile = best_tile(tile[...], 1, sums, inside_rows(place, info, variants))
    lane = lax.broadcasted_iota(jnp.int32, (HALF, LANES), 1)
    row = lax.broadcasted_iota(jnp.int32, (HALF, LANES), 0)
    keep = ((lane < 96) & (lane % HALF == row)) | ((lane >= 96) & (row == 0))
    line = jnp.sum(jnp.where(keep, tile, 0.0), axis=0, keepdims=True)
    for i in range(out.shape[0] // HALF):
        out[i * HALF : (i + 1) * HALF, :] = jnp.broadcast_to(line, (HALF, LANES))


def final_kernel(place, order, parts, out, observed, store):
    shards = HALF
    owners = parts.shape[0] // shards
    block = lambda o: parts[o * shards : (o + 1) * shards, :]
    width = 2 * HALF
    for o in range(owners):
        best = block(o)
        if o > 0:
            best = jnp.maximum(best, pltpu.roll(block(o - 1), LANES - 2 * width, 1))
        if o < owners - 1:
            best = jnp.maximum(best, pltpu.roll(block(o + 1), 2 * width, 1))
        store[2 * o] = best
        store[2 * o + 1] = pltpu.roll(best, LANES - width, 1)
    g = place[0]
    zero = jnp.zeros((shards, LANES), jnp.float32)
    tails = [zero, zero]
    for i in range(2 * owners):
        value = store[order[i]]
        for k in range(2):
            tails[k] = jnp.where(i >= 2 * g + k, jnp.maximum(tails[k], value), tails[k])
    lane = lax.broadcasted_iota(jnp.int32, (shards, LANES), 1)
    row = lax.broadcasted_iota(jnp.int32, (shards, LANES), 0)
    for k in range(2):
        moved = pltpu.roll(tails[k], LANES - 2 * width, 1)
        moved = pltpu.roll(moved, 0, 1, stride=width, stride_axis=0)
        out[k : k + 1, :] = jnp.sum(
            jnp.where(lane // width == row, moved, 0.0), axis=0, keepdims=True
        )
    part = lambda o: parts[pl.ds(pl.multiple_of(o * shards, shards), shards), :][:1]
    seen = part(g)
    left = pltpu.roll(part(jnp.maximum(g - 1, 0)), LANES - 2, 1)
    right = pltpu.roll(part(jnp.minimum(g + 1, owners - 1)), 2, 1)
    seen = jnp.maximum(seen, jnp.where(g > 0, left, 0.0))
    seen = jnp.maximum(seen, jnp.where(g < owners - 1, right, 0.0))
    observed[...] = seen[:, 98:100]


def call(kernel, outs, args, us, scratch=(), remote=()):
    scalar = [a.size <= 64 for a in args]
    many = isinstance(outs, list)
    made = pl.pallas_call(
        kernel,
        out_shape=tuple(outs) if many else outs,
        in_specs=[
            pl.BlockSpec(memory_space=pltpu.HBM) if i in remote else SM if k else VM
            for i, k in enumerate(scalar)
        ],
        out_specs=tuple([VM] * len(outs))
        if many
        else pl.BlockSpec(memory_space=pltpu.HBM)
        if remote
        else VM,
        scratch_shapes=scratch,
        compiler_params=pltpu.CompilerParams(vmem_limit_bytes=24 << 20),
        cost_estimate=pl.CostEstimate(flops=int(us * 1e9), bytes_accessed=0, transcendentals=0),
    )
    args = [
        a
        if k
        else pltpu.with_memory_space_constraint(a, pltpu.HBM if i in remote else pltpu.VMEM)
        for i, (a, k) in enumerate(zip(args, scalar))
    ]
    return made(*args)


def shape(dims, kind=jnp.float32):
    return pltpu.VMEM(dims, kind)


def on_device(dosage, expression, perms, windows, order):
    variants, width = dosage.shape
    owners = lax.axis_size("gene")
    shards = 8
    samples = width * shards
    g, z, c = lax.axis_index("gene"), lax.axis_index("z"), lax.axis_index("core")
    place = jnp.stack([g, z, c]).astype(jnp.int32)
    mates = [(0, 1), (1, 0)]
    their_perms = lax.ppermute(perms, "core", mates)
    theirs = lax.ppermute(dosage, "core", mates)
    copies = call(
        copies_kernel,
        pltpu.HBM((shards, 2, width), jnp.float32),
        [expression.T],
        1,
        [pltpu.SemaphoreType.DMA((shards,))],
        remote=(0,),
    )
    every = lax.all_to_all(copies, ("z", "core"), 0, 0, tiled=True)
    stat = call(
        moments_kernel,
        shape((8, variants)),
        [dosage, theirs],
        2,
        [pltpu.VMEM((2, variants, LANES), jnp.float32)],
    )

    table_shape = shape((2, samples // LANES, TILE, LANES), jnp.bfloat16)
    first, table = call(
        first_kernel,
        [shape((5 * TILE, 2 * width), jnp.bfloat16), table_shape],
        [place, windows, every, perms, their_perms],
        9,
    )
    second = call(
        functools.partial(later_kernel, 1),
        shape((4 * TILE, 2 * width), jnp.bfloat16),
        [place, perms, their_perms, table],
        8,
    )
    ahead = [(i, (i + 1) % owners) for i in range(owners)]
    back = [(b, a) for a, b in ahead]
    sums = []
    for h, own in enumerate((first, second)):
        left = lax.ppermute(own, "gene", ahead)
        right = lax.ppermute(own, "gene", back)
        depth, deep = (56, 64) if h == 0 else (48, 48)
        outs = [shape((depth, variants))] + [shape((deep, variants + LANES), jnp.int16)] * 3
        own, *parts = call(
            functools.partial(sums_kernel, h),
            outs + ([shape((8, LANES))] if h == 0 else []),
            [left, own, right, dosage, theirs, stat],
            2,
        )
        if h == 0:
            info = parts.pop()
        group = [own]
        for k in range(1, 4):
            group.append(lax.ppermute(parts[k - 1], "z", [(i, (i + k) % 4) for i in range(4)]))
        sums.append(group)
    tile, aux = call(
        functools.partial(early_kernel, samples),
        [shape((HALF, LANES)), shape((8, variants))],
        [place, info, stat, *sums[0]],
        1,
    )
    everyone = owners * shards
    lines = call(maxima_kernel, shape((everyone, LANES)), [place, info, aux, tile, *sums[1]], 2)
    lines = lax.all_to_all(
        lines.reshape(everyone, 1, LANES), ("gene", "z", "core"), 0, 0, tiled=True
    ).reshape(everyone, LANES)
    successive, observed = call(
        final_kernel,
        [jax.ShapeDtypeStruct((2, LANES), jnp.float32), jax.ShapeDtypeStruct((1, 2), jnp.float32)],
        [place, order, lines],
        2,
        [pltpu.VMEM((2 * owners, HALF, LANES), jnp.float32)],
    )
    return observed.reshape(2), successive


def solution(mesh):
    split = Mesh(mesh.devices.reshape(16, 4, 2), ("gene", "z", "core"))
    samp = ("z", "core")
    placed = (P("gene", samp), P(samp, "gene"), P(None, samp), P("gene", None), P())
    return jax.shard_map(
        on_device,
        mesh=split,
        in_specs=placed,
        out_specs=(P("gene"), P("gene", None)),
        check_vma=False,
    )
```

```python
import functools

import jax
import jax.numpy as jnp
from jax import lax
from jax.experimental import pallas as pl
from jax.experimental.pallas import tpu as pltpu
from jax.sharding import Mesh
from jax.sharding import PartitionSpec as P


epsilon = 1e-06
LANES = 128
TILE = 16
HALF = 8
CHUNKS = 2

VM = pl.BlockSpec(memory_space=pltpu.VMEM)
SM = pl.BlockSpec(memory_space=pltpu.SMEM)


def lane_gather(table, index):
    dims = lax.GatherDimensionNumbers(
        offset_dims=(),
        collapsed_slice_dims=(1,),
        start_index_map=(1,),
        operand_batching_dims=(0,),
        start_indices_batching_dims=(0,),
    )
    return lax.gather(
        table,
        index[..., None],
        dims,
        slice_sizes=(1, 1),
        mode=lax.GatherScatterMode.PROMISE_IN_BOUNDS,
    )


def look_up(chunk, genes, place, perms, theirs, table, out):
    z, c = place[1], place[2]
    table_rows = table.shape[1]
    width = perms.shape[1]

    def step(pair, carry):
        first = []
        for k in range(2):
            d = lax.rem(z + pair * 2 + k, 4) * 2 + c
            first.append(pl.multiple_of(d * 2 * HALF + chunk * HALF, HALF))
        for u in range(2 * width // LANES):
            source = perms if u < width // LANES else theirs
            lane = u % (width // LANES) * LANES
            rows = [source[pl.ds(f, HALF), lane : lane + LANES] for f in first]
            index = jnp.concatenate(rows, axis=0)
            low = (index & (LANES - 1)).astype(jnp.int16)
            high = (index >> 7).astype(jnp.int16)
            found = [jnp.zeros((TILE, LANES), jnp.bfloat16) for _ in genes]
            for r in range(table_rows):
                here = high == jnp.int16(r)
                for n, j in enumerate(genes):
                    found[n] = jnp.where(here, lane_gather(table[j, r], low), found[n])
            for n in range(len(genes)):
                row = pl.multiple_of(n * 2 * TILE + pair * TILE, TILE)
                out[pl.ds(row, TILE), u * LANES : (u + 1) * LANES] = found[n]
        return carry

    lax.fori_loop(0, 2, step, 0)


def lane_sums(rows):
    return lax.dot_general(
        jnp.ones((8, LANES), jnp.float32),
        rows,
        (((1,), (1,)), ((), ())),
        precision=lax.Precision.HIGHEST,
        preferred_element_type=jnp.float32,
    )[:1]


def moments_kernel(dosage, out, sums):
    variants, width = dosage.shape

    def step(i, carry):
        rows = pl.ds(pl.multiple_of(i * LANES, LANES), LANES)
        total = jnp.zeros((LANES, LANES), jnp.float32)
        square = jnp.zeros((LANES, LANES), jnp.float32)
        for k in range(width // LANES):
            v = dosage[rows, k * LANES : (k + 1) * LANES].astype(jnp.float32)
            total = total + v
            square = square + v * v
        sums[0, rows, :] = total
        sums[1, rows, :] = square
        return carry

    lax.fori_loop(0, variants // LANES, step, 0)
    out[...] = jnp.zeros_like(out)
    for j in range(2):
        out[j : j + 1, :] = lane_sums(sums[j])


def first_kernel(place, windows, every, perms, theirs, out, table):
    z, c = place[1], place[2]
    shards, genes, width = every.shape
    samples = shards * width
    own = jnp.concatenate([every[z * 2 + c], every[z * 2 + 1 - c]], axis=1)
    direct = []
    for j in range(genes):
        x = every[:, j, :]
        mean = jnp.sum(x, keepdims=True) / samples
        center = x - mean
        scale = lax.rsqrt(jnp.sum(center * center, keepdims=True) / samples + epsilon)
        scaled = center * scale
        for k in range(shards):
            for i in range(width // LANES):
                piece = scaled[k : k + 1, i * LANES : (i + 1) * LANES]
                table[j, k * (width // LANES) + i] = jnp.broadcast_to(piece, (TILE, LANES)).astype(
                    jnp.bfloat16
                )
        direct.append((own[j : j + 1] - mean) * scale)
    tiles = 2 * width // LANES
    lines = [direct[j][:, t * LANES : (t + 1) * LANES] for j in range(genes) for t in range(tiles)]
    lane = lax.broadcasted_iota(jnp.int32, (1, LANES), 1)
    for d in range(2):
        line = jnp.zeros((1, LANES), jnp.float32)
        for j in range(genes):
            for b in range(2):
                w = windows[j, b]
                digit = (w & 127) if d else (w >> 7)
                line = jnp.where(lane == j * 2 + b, digit.astype(jnp.float32), line)
        lines.append(line)
    lines.append(jnp.zeros((4 * TILE - len(lines), LANES), jnp.float32))
    out[:, 2 * width :] = jnp.concatenate(lines, axis=0).astype(jnp.bfloat16)
    look_up(0, (0, 1), place, perms, theirs, table, out)


def later_kernel(chunk, place, perms, theirs, table, out):
    look_up(chunk, (0, 1), place, perms, theirs, table, out)


def times(rows, dosage):
    return lax.dot_general(
        rows, dosage, (((1,), (1,)), ((), ())), preferred_element_type=jnp.float32
    )


LEVELS = 32767.0
PARTS = 256.0


def bound_code(largest):
    return jnp.clip(jnp.ceil(largest * PARTS), 1.0, LEVELS)


def coded(values, code):
    scaled = values * (LEVELS * PARTS / code)
    return jnp.clip(jnp.round(scaled), -LEVELS, LEVELS)


def to_int16(values):
    return values.astype(jnp.int32).astype(jnp.int16)


def digits(x):
    whole = jnp.floor(x)
    rest = (x - whole) * 32768.0
    high = jnp.floor(rest)
    return whole, high, jnp.floor((rest - high) * 32768.0)


def undigits(whole, high, low):
    return whole + (high + low * (1.0 / 32768.0)) * (1.0 / 32768.0)


def mean_and_size(total, square, count):
    mean = total / count
    return mean, jnp.sqrt(jnp.maximum(square - total * mean, 0.0) + count * epsilon)


def sums_kernel(chunk, *refs):
    blocks = refs[:3]
    dosage, theirs, stat, their_stat, own, m1, m2, m3 = refs[3:11]
    variants, width = dosage.shape
    stat = stat[...] + their_stat[...]
    rows = jnp.concatenate([block[:, : 2 * width] for block in blocks], axis=0)
    if chunk == 0:
        tiles = 2 * width // LANES
        extra = [block[:, 2 * width :].astype(jnp.float32) for block in blocks]
        direct = [
            jnp.concatenate([e[j * tiles + t : j * tiles + t + 1] for t in range(tiles)], axis=1)
            for e in extra
            for j in range(2)
        ]
        direct.append(jnp.zeros((TILE - 6, 2 * width), jnp.float32))
        rows = jnp.concatenate([rows, jnp.concatenate(direct, axis=0).astype(jnp.bfloat16)], axis=0)
    both = times(rows[:, :width], dosage[...]) + times(rows[:, width:], theirs[...])
    column = jnp.sum(rows.astype(jnp.float32), axis=1, keepdims=True)
    mean, size = mean_and_size(stat[0:1, :], stat[1:2, :], 2.0 * width)
    got = (both - column * mean) * (1.0 / size)
    column = jnp.broadcast_to(column, (column.shape[0], LANES))
    at = lambda n, kz: slice(n * 2 * TILE + kz * HALF, n * 2 * TILE + (kz + 1) * HALF)
    for n in range(6):
        own[n * HALF : (n + 1) * HALF, :] = both[at(n, 0)]
    largest = jnp.abs(got[at(0, 1)])
    for n in range(6):
        for kz in range(1, 4):
            largest = jnp.maximum(largest, jnp.abs(got[at(n, kz)]))

    def beside(code, columns):
        lane = lax.broadcasted_iota(jnp.int32, columns.shape, 1)
        whole, high, low = digits(columns)
        line = jnp.where(lane == 1, whole, jnp.where(lane == 2, high, low))
        return to_int16(jnp.where(lane == 0, code, line))

    code = bound_code(jnp.max(largest, keepdims=True))
    for k, message in enumerate((m1, m2, m3)):
        for t in range(3):
            pair = [at(2 * t, k + 1), at(2 * t + 1, k + 1)]
            values = jnp.concatenate([got[p] for p in pair], axis=0)
            columns = jnp.concatenate([column[p] for p in pair], axis=0)
            message[t * TILE : (t + 1) * TILE, :variants] = to_int16(coded(values, code))
            message[t * TILE : (t + 1) * TILE, variants:] = beside(code, columns)
    if chunk == 0:
        spots = slice(12 * TILE, 12 * TILE + HALF)
        own[48:56, :] = both[spots]
        values, columns = got[spots], column[spots]
        code = bound_code(jnp.max(jnp.abs(values), keepdims=True))
        rest = list(digits(stat[0:1, :]) + digits(stat[1:2, :]))
        rest.append(jnp.zeros((2, variants), jnp.float32))
        tail = to_int16(jnp.concatenate([coded(values, code)] + rest, axis=0))
        side = beside(code, jnp.concatenate([columns, jnp.zeros_like(columns)], axis=0))
        for message in (m1, m2, m3):
            message[48:64, :variants] = tail
            message[48:64, variants:] = side
        info = refs[-1]
        info[...] = jnp.zeros_like(info)
        for o, e in enumerate(extra):
            info[o : o + 1, :] = e[2 * tiles : 2 * tiles + 1] * 128.0 + e[2 * tiles + 1 : 2 * tiles + 2]


def added(own, messages, means, sizes):
    total = own[...]
    rows, variants = total.shape
    for message, mean, size in zip(messages, means, sizes):
        side = message[:rows, variants:].astype(jnp.int32).astype(jnp.float32)
        column = undigits(side[:, 1:2], side[:, 2:3], side[:, 3:4])
        unit = side[:, 0:1] * (1.0 / (LEVELS * PARTS))
        codes = message[:rows, :variants].astype(jnp.int32).astype(jnp.float32)
        total = total + (codes * unit * size + column * mean)
    return total


def inside_rows(place, info, variants):
    index = lax.broadcasted_iota(jnp.int32, (1, variants), 1) + place[0] * variants
    index = index.astype(jnp.float32)
    for o in range(3):
        for j in range(2):
            lo = info[o : o + 1, j * 2 : j * 2 + 1]
            hi = info[o : o + 1, j * 2 + 1 : j * 2 + 2]
            yield (index >= lo) & (index < hi)


def best_tile(tile, h, total, inside):
    lane = lax.broadcasted_iota(jnp.int32, (HALF, LANES), 1)
    for n, mask in enumerate(inside):
        v = jnp.abs(total[n * HALF : (n + 1) * HALF])
        best = jnp.max(jnp.where(mask, v, 0.0), axis=1, keepdims=True)
        tile = jnp.where(lane // HALF == n * CHUNKS + h, best, tile)
    return tile


def early_kernel(samples, place, info, stat, their_stat, own, m1, m2, m3, out, aux):
    variants = own.shape[1]
    count = samples / 4.0
    stat = stat[...] + their_stat[...]
    total, square = stat[0:1, :], stat[1:2, :]
    means, sizes = [], []
    for message in (m1, m2, m3):
        d = message[48:64, :variants].astype(jnp.int32).astype(jnp.float32)
        their_total = undigits(d[8:9], d[9:10], d[10:11])
        their_square = undigits(d[11:12], d[12:13], d[13:14])
        mean, size = mean_and_size(their_total, their_square, count)
        means.append(mean)
        sizes.append(size)
        total = total + their_total
        square = square + their_square
    row_mean = total / samples
    spread = square / samples - row_mean * row_mean + epsilon
    scale = lax.rsqrt(spread * samples)
    aux[0:1, :] = scale
    for q in range(3):
        aux[1 + q : 2 + q, :] = means[q]
        aux[4 + q : 5 + q, :] = sizes[q]
    aux[7:8, :] = jnp.zeros_like(scale)
    sums = added(own, (m1, m2, m3), means, sizes) * scale
    inside = list(inside_rows(place, info, variants))
    tile = best_tile(jnp.zeros((HALF, LANES), jnp.float32), 0, sums, inside)
    lane = lax.broadcasted_iota(jnp.int32, (HALF, LANES), 1)
    for n, mask in enumerate(inside):
        v = jnp.abs(sums[48 + n : 49 + n])
        best = jnp.max(jnp.where(mask, v, 0.0), axis=1, keepdims=True)
        tile = jnp.where(lane == 96 + n, best, tile)
    out[...] = tile


def maxima_kernel(place, info, aux, tile, own, m1, m2, m3, out):
    variants = own.shape[1]
    means = [aux[1 + q : 2 + q, :] for q in range(3)]
    sizes = [aux[4 + q : 5 + q, :] for q in range(3)]
    sums = added(own, (m1, m2, m3), means, sizes) * aux[0:1, :]
    tile = best_tile(tile[...], 1, sums, inside_rows(place, info, variants))
    lane = lax.broadcasted_iota(jnp.int32, (HALF, LANES), 1)
    row = lax.broadcasted_iota(jnp.int32, (HALF, LANES), 0)
    keep = ((lane < 96) & (lane % HALF == row)) | ((lane >= 96) & (row == 0))
    line = jnp.sum(jnp.where(keep, tile, 0.0), axis=0, keepdims=True)
    for i in range(out.shape[0] // HALF):
        out[i * HALF : (i + 1) * HALF, :] = jnp.broadcast_to(line, (HALF, LANES))


def final_kernel(place, order, parts, out, observed, store):
    shards = HALF
    owners = parts.shape[0] // shards
    block = lambda o: parts[o * shards : (o + 1) * shards, :]
    width = 2 * HALF
    for o in range(owners):
        best = block(o)
        if o > 0:
            best = jnp.maximum(best, pltpu.roll(block(o - 1), LANES - 2 * width, 1))
        if o < owners - 1:
            best = jnp.maximum(best, pltpu.roll(block(o + 1), 2 * width, 1))
        store[2 * o] = best
        store[2 * o + 1] = pltpu.roll(best, LANES - width, 1)
    g = place[0]
    zero = jnp.zeros((shards, LANES), jnp.float32)
    tails = [zero, zero]
    for i in range(2 * owners):
        value = store[order[i]]
        for k in range(2):
            tails[k] = jnp.where(i >= 2 * g + k, jnp.maximum(tails[k], value), tails[k])
    lane = lax.broadcasted_iota(jnp.int32, (shards, LANES), 1)
    row = lax.broadcasted_iota(jnp.int32, (shards, LANES), 0)
    for k in range(2):
        moved = pltpu.roll(tails[k], LANES - 2 * width, 1)
        moved = pltpu.roll(moved, 0, 1, stride=width, stride_axis=0)
        out[k : k + 1, :] = jnp.sum(
            jnp.where(lane // width == row, moved, 0.0), axis=0, keepdims=True
        )
    part = lambda o: parts[pl.ds(pl.multiple_of(o * shards, shards), shards), :][:1]
    seen = part(g)
    left = pltpu.roll(part(jnp.maximum(g - 1, 0)), LANES - 2, 1)
    right = pltpu.roll(part(jnp.minimum(g + 1, owners - 1)), 2, 1)
    seen = jnp.maximum(seen, jnp.where(g > 0, left, 0.0))
    seen = jnp.maximum(seen, jnp.where(g < owners - 1, right, 0.0))
    observed[...] = seen[:, 98:100]


def call(kernel, outs, args, us, scratch=(), remote=()):
    scalar = [a.size <= 64 for a in args]
    many = isinstance(outs, list)
    made = pl.pallas_call(
        kernel,
        out_shape=tuple(outs) if many else outs,
        in_specs=[
            pl.BlockSpec(memory_space=pltpu.HBM) if i in remote else SM if k else VM
            for i, k in enumerate(scalar)
        ],
        out_specs=tuple([VM] * len(outs))
        if many
        else pl.BlockSpec(memory_space=pltpu.HBM)
        if remote
        else VM,
        scratch_shapes=scratch,
        compiler_params=pltpu.CompilerParams(vmem_limit_bytes=24 << 20),
        cost_estimate=pl.CostEstimate(flops=int(us * 1e9), bytes_accessed=0, transcendentals=0),
    )
    args = [
        a
        if k
        else pltpu.with_memory_space_constraint(a, pltpu.HBM if i in remote else pltpu.VMEM)
        for i, (a, k) in enumerate(zip(args, scalar))
    ]
    return made(*args)


def shape(dims, kind=jnp.float32):
    return pltpu.VMEM(dims, kind)


def on_device(dosage, expression, perms, windows, order):
    variants, width = dosage.shape
    owners = lax.axis_size("gene")
    shards = 8
    samples = width * shards
    g, z, c = lax.axis_index("gene"), lax.axis_index("z"), lax.axis_index("core")
    place = jnp.stack([g, z, c]).astype(jnp.int32)
    copies = jnp.broadcast_to(expression.T[None], (shards, 2, width))
    every = lax.all_to_all(copies, ("z", "core"), 0, 0, tiled=True)
    mates = [(0, 1), (1, 0)]
    their_perms = lax.ppermute(perms, "core", mates)
    theirs = lax.ppermute(dosage, "core", mates)
    stat = call(
        moments_kernel,
        shape((8, variants)),
        [dosage],
        2,
        [pltpu.VMEM((2, variants, LANES), jnp.float32)],
    )
    their_stat = lax.ppermute(stat, "core", mates)

    table_shape = shape((2, samples // LANES, TILE, LANES), jnp.bfloat16)
    first, table = call(
        first_kernel,
        [shape((4 * TILE, 2 * width + LANES), jnp.bfloat16), table_shape],
        [place, windows, every, perms, their_perms],
        9,
    )
    second = call(
        functools.partial(later_kernel, 1),
        shape((4 * TILE, 2 * width), jnp.bfloat16),
        [place, perms, their_perms, table],
        8,
    )
    ahead = [(i, (i + 1) % owners) for i in range(owners)]
    back = [(b, a) for a, b in ahead]
    sums = []
    for h, own in enumerate((first, second)):
        left = lax.ppermute(own, "gene", ahead)
        right = lax.ppermute(own, "gene", back)
        depth, deep = (56, 64) if h == 0 else (48, 48)
        outs = [shape((depth, variants))] + [shape((deep, variants + LANES), jnp.int16)] * 3
        own, *parts = call(
            functools.partial(sums_kernel, h),
            outs + ([shape((8, LANES))] if h == 0 else []),
            [left, own, right, dosage, theirs, stat, their_stat],
            2,
        )
        if h == 0:
            info = parts.pop()
        group = [own]
        for k in range(1, 4):
            group.append(lax.ppermute(parts[k - 1], "z", [(i, (i + k) % 4) for i in range(4)]))
        sums.append(group)
    tile, aux = call(
        functools.partial(early_kernel, samples),
        [shape((HALF, LANES)), shape((8, variants))],
        [place, info, stat, their_stat, *sums[0]],
        1,
    )
    everyone = owners * shards
    lines = call(maxima_kernel, shape((everyone, LANES)), [place, info, aux, tile, *sums[1]], 2)
    lines = lax.all_to_all(
        lines.reshape(everyone, 1, LANES), ("gene", "z", "core"), 0, 0, tiled=True
    ).reshape(everyone, LANES)
    successive, observed = call(
        final_kernel,
        [jax.ShapeDtypeStruct((2, LANES), jnp.float32), jax.ShapeDtypeStruct((1, 2), jnp.float32)],
        [place, order, lines],
        2,
        [pltpu.VMEM((2 * owners, HALF, LANES), jnp.float32)],
    )
    return observed.reshape(2), successive


def solution(mesh):
    split = Mesh(mesh.devices.reshape(16, 4, 2), ("gene", "z", "core"))
    samp = ("z", "core")
    placed = (P("gene", samp), P(samp, "gene"), P(None, samp), P("gene", None), P())
    return jax.shard_map(
        on_device,
        mesh=split,
        in_specs=placed,
        out_specs=(P("gene"), P("gene", None)),
        check_vma=False,
    )
```

```python
import functools

import jax
import jax.numpy as jnp
from jax import lax
from jax.experimental import pallas as pl
from jax.experimental.pallas import tpu as pltpu
from jax.sharding import Mesh
from jax.sharding import PartitionSpec as P


epsilon = 1e-06
LANES = 128
TILE = 16
HALF = 8
CHUNKS = 2

VM = pl.BlockSpec(memory_space=pltpu.VMEM)
SM = pl.BlockSpec(memory_space=pltpu.SMEM)


def lane_gather(table, index):
    dims = lax.GatherDimensionNumbers(
        offset_dims=(),
        collapsed_slice_dims=(1,),
        start_index_map=(1,),
        operand_batching_dims=(0,),
        start_indices_batching_dims=(0,),
    )
    return lax.gather(
        table,
        index[..., None],
        dims,
        slice_sizes=(1, 1),
        mode=lax.GatherScatterMode.PROMISE_IN_BOUNDS,
    )


def look_up(chunk, place, perms, theirs, table, out):
    z, c = place[1], place[2]
    genes, table_rows = table.shape[:2]
    width = perms.shape[1]
    group = 5
    steps = width // LANES // group
    zero = jnp.zeros((TILE, LANES), jnp.bfloat16)
    for s, source in enumerate((perms, theirs)):

        def step(t, carry, s=s, source=source):
            pair, part = t // steps, t % steps
            first = []
            for k in range(2):
                d = lax.rem(z + pair * 2 + k, 4) * 2 + c
                first.append(pl.multiple_of(d * 2 * HALF + chunk * HALF, HALF))
            found = [zero] * genes
            for u in range(group):
                lane = pl.multiple_of((part * group + u) * LANES, LANES)
                index = jnp.concatenate(
                    [source[pl.ds(f, HALF), pl.ds(lane, LANES)] for f in first], axis=0
                )
                low = (index & (LANES - 1)).astype(jnp.int16)
                high = (index >> 7).astype(jnp.int16)
                never = high < jnp.int16(0)
                found = [jnp.where(never, f, zero) for f in found]
                for r in range(table_rows):
                    here = high == jnp.int16(r)
                    for j in range(genes):
                        found[j] = jnp.where(here, lane_gather(table[j, r], low), found[j])
                    if r % 16 == 0:
                        found = [
                            jnp.where(never, found[genes - 1 - j], found[j]) for j in range(genes)
                        ]
                for j in range(genes):
                    row = pl.multiple_of(j * 2 * TILE + pair * TILE, TILE)
                    to = pl.multiple_of(lane + s * width, LANES)
                    out[pl.ds(row, TILE), pl.ds(to, LANES)] = found[j]
            return carry

        lax.fori_loop(0, 2 * steps, step, 0)


def lane_sums(rows):
    return lax.dot_general(
        jnp.ones((8, LANES), jnp.float32),
        rows,
        (((1,), (1,)), ((), ())),
        precision=lax.Precision.HIGHEST,
        preferred_element_type=jnp.float32,
    )[:1]


def fetch_kernel(source, out, done):
    copy = pltpu.make_async_copy(source, out, done)
    copy.start()
    copy.wait()


def moments_kernel(dosage, out, sums):
    variants, width = dosage.shape

    def step(i, carry):
        rows = pl.ds(pl.multiple_of(i * LANES, LANES), LANES)
        total = jnp.zeros((LANES, LANES), jnp.float32)
        square = jnp.zeros((LANES, LANES), jnp.float32)
        for k in range(width // LANES):
            v = dosage[rows, k * LANES : (k + 1) * LANES].astype(jnp.float32)
            total = total + v
            square = square + v * v
        sums[0, rows, :] = total
        sums[1, rows, :] = square
        return carry

    lax.fori_loop(0, variants // LANES, step, 0)
    out[...] = jnp.zeros_like(out)
    for j in range(2):
        out[j : j + 1, :] = lane_sums(sums[j])


def first_kernel(place, windows, every, perms, theirs, out, table):
    z, c = place[1], place[2]
    shards, genes, width = every.shape
    samples = shards * width
    own = jnp.concatenate([every[z * 2 + c], every[z * 2 + 1 - c]], axis=1)
    direct = []
    for j in range(genes):
        x = every[:, j, :]
        mean = jnp.sum(x, keepdims=True) / samples
        center = x - mean
        scale = lax.rsqrt(jnp.sum(center * center, keepdims=True) / samples + epsilon)
        scaled = center * scale
        for k in range(shards):
            for i in range(width // LANES):
                piece = scaled[k : k + 1, i * LANES : (i + 1) * LANES]
                table[j, k * (width // LANES) + i] = jnp.broadcast_to(piece, (TILE, LANES)).astype(
                    jnp.bfloat16
                )
        direct.append((own[j : j + 1] - mean) * scale)
    tiles = 2 * width // LANES
    lines = [direct[j][:, t * LANES : (t + 1) * LANES] for j in range(genes) for t in range(tiles)]
    lane = lax.broadcasted_iota(jnp.int32, (1, LANES), 1)
    for d in range(2):
        line = jnp.zeros((1, LANES), jnp.float32)
        for j in range(genes):
            for b in range(2):
                w = windows[j, b]
                digit = (w & 127) if d else (w >> 7)
                line = jnp.where(lane == j * 2 + b, digit.astype(jnp.float32), line)
        lines.append(line)
    lines.append(jnp.zeros((4 * TILE - len(lines), LANES), jnp.float32))
    out[:, 2 * width :] = jnp.concatenate(lines, axis=0).astype(jnp.bfloat16)
    look_up(0, place, perms, theirs, table, out)


def later_kernel(chunk, place, perms, theirs, table, out):
    look_up(chunk, place, perms, theirs, table, out)


def times(rows, dosage):
    return lax.dot_general(
        rows, dosage, (((1,), (1,)), ((), ())), preferred_element_type=jnp.float32
    )


LEVELS = 32767.0
PARTS = 256.0


def bound_code(largest):
    return jnp.clip(jnp.ceil(largest * PARTS), 1.0, LEVELS)


def coded(values, code):
    scaled = values * (LEVELS * PARTS / code)
    return jnp.clip(jnp.round(scaled), -LEVELS, LEVELS)


def to_int16(values):
    return values.astype(jnp.int32).astype(jnp.int16)


def digits(x):
    whole = jnp.floor(x)
    rest = (x - whole) * 32768.0
    high = jnp.floor(rest)
    return whole, high, jnp.floor((rest - high) * 32768.0)


def undigits(whole, high, low):
    return whole + (high + low * (1.0 / 32768.0)) * (1.0 / 32768.0)


def mean_and_size(total, square, count):
    mean = total / count
    return mean, jnp.sqrt(jnp.maximum(square - total * mean, 0.0) + count * epsilon)


def sums_kernel(chunk, *refs):
    blocks = refs[:3]
    dosage, theirs, stat, their_stat, own, m1, m2, m3 = refs[3:11]
    variants, width = dosage.shape
    stat = stat[...] + their_stat[...]
    rows = jnp.concatenate([block[:, : 2 * width] for block in blocks], axis=0)
    if chunk == 0:
        tiles = 2 * width // LANES
        extra = [block[:, 2 * width :].astype(jnp.float32) for block in blocks]
        direct = [
            jnp.concatenate([e[j * tiles + t : j * tiles + t + 1] for t in range(tiles)], axis=1)
            for e in extra
            for j in range(2)
        ]
        direct.append(jnp.zeros((TILE - 6, 2 * width), jnp.float32))
        rows = jnp.concatenate([rows, jnp.concatenate(direct, axis=0).astype(jnp.bfloat16)], axis=0)
    both = times(rows[:, :width], dosage[...]) + times(rows[:, width:], theirs[...])
    column = jnp.sum(rows.astype(jnp.float32), axis=1, keepdims=True)
    mean, size = mean_and_size(stat[0:1, :], stat[1:2, :], 2.0 * width)
    got = (both - column * mean) * (1.0 / size)
    column = jnp.broadcast_to(column, (column.shape[0], LANES))
    at = lambda n, kz: slice(n * 2 * TILE + kz * HALF, n * 2 * TILE + (kz + 1) * HALF)
    for n in range(6):
        own[n * HALF : (n + 1) * HALF, :] = both[at(n, 0)]
    largest = jnp.abs(got[at(0, 1)])
    for n in range(6):
        for kz in range(1, 4):
            largest = jnp.maximum(largest, jnp.abs(got[at(n, kz)]))

    def beside(code, columns):
        lane = lax.broadcasted_iota(jnp.int32, columns.shape, 1)
        whole, high, low = digits(columns)
        line = jnp.where(lane == 1, whole, jnp.where(lane == 2, high, low))
        return to_int16(jnp.where(lane == 0, code, line))

    code = bound_code(jnp.max(largest, keepdims=True))
    for k, message in enumerate((m1, m2, m3)):
        for t in range(3):
            pair = [at(2 * t, k + 1), at(2 * t + 1, k + 1)]
            values = jnp.concatenate([got[p] for p in pair], axis=0)
            columns = jnp.concatenate([column[p] for p in pair], axis=0)
            message[t * TILE : (t + 1) * TILE, :variants] = to_int16(coded(values, code))
            message[t * TILE : (t + 1) * TILE, variants:] = beside(code, columns)
    if chunk == 0:
        spots = slice(12 * TILE, 12 * TILE + HALF)
        own[48:56, :] = both[spots]
        values, columns = got[spots], column[spots]
        code = bound_code(jnp.max(jnp.abs(values), keepdims=True))
        rest = list(digits(stat[0:1, :]) + digits(stat[1:2, :]))
        rest.append(jnp.zeros((2, variants), jnp.float32))
        tail = to_int16(jnp.concatenate([coded(values, code)] + rest, axis=0))
        side = beside(code, jnp.concatenate([columns, jnp.zeros_like(columns)], axis=0))
        for message in (m1, m2, m3):
            message[48:64, :variants] = tail
            message[48:64, variants:] = side
        info = refs[-1]
        info[...] = jnp.zeros_like(info)
        for o, e in enumerate(extra):
            info[o : o + 1, :] = e[2 * tiles : 2 * tiles + 1] * 128.0 + e[2 * tiles + 1 : 2 * tiles + 2]


def added(own, messages, means, sizes):
    total = own[...]
    rows, variants = total.shape
    for message, mean, size in zip(messages, means, sizes):
        side = message[:rows, variants:].astype(jnp.int32).astype(jnp.float32)
        column = undigits(side[:, 1:2], side[:, 2:3], side[:, 3:4])
        unit = side[:, 0:1] * (1.0 / (LEVELS * PARTS))
        codes = message[:rows, :variants].astype(jnp.int32).astype(jnp.float32)
        total = total + (codes * unit * size + column * mean)
    return total


def inside_rows(place, info, variants):
    index = lax.broadcasted_iota(jnp.int32, (1, variants), 1) + place[0] * variants
    index = index.astype(jnp.float32)
    for o in range(3):
        for j in range(2):
            lo = info[o : o + 1, j * 2 : j * 2 + 1]
            hi = info[o : o + 1, j * 2 + 1 : j * 2 + 2]
            yield (index >= lo) & (index < hi)


def best_tile(tile, h, total, inside):
    lane = lax.broadcasted_iota(jnp.int32, (HALF, LANES), 1)
    for n, mask in enumerate(inside):
        v = jnp.abs(total[n * HALF : (n + 1) * HALF])
        best = jnp.max(jnp.where(mask, v, 0.0), axis=1, keepdims=True)
        tile = jnp.where(lane // HALF == n * CHUNKS + h, best, tile)
    return tile


def early_kernel(samples, place, info, stat, their_stat, own, m1, m2, m3, out, aux):
    variants = own.shape[1]
    count = samples / 4.0
    stat = stat[...] + their_stat[...]
    total, square = stat[0:1, :], stat[1:2, :]
    means, sizes = [], []
    for message in (m1, m2, m3):
        d = message[48:64, :variants].astype(jnp.int32).astype(jnp.float32)
        their_total = undigits(d[8:9], d[9:10], d[10:11])
        their_square = undigits(d[11:12], d[12:13], d[13:14])
        mean, size = mean_and_size(their_total, their_square, count)
        means.append(mean)
        sizes.append(size)
        total = total + their_total
        square = square + their_square
    row_mean = total / samples
    spread = square / samples - row_mean * row_mean + epsilon
    scale = lax.rsqrt(spread * samples)
    aux[0:1, :] = scale
    for q in range(3):
        aux[1 + q : 2 + q, :] = means[q]
        aux[4 + q : 5 + q, :] = sizes[q]
    aux[7:8, :] = jnp.zeros_like(scale)
    sums = added(own, (m1, m2, m3), means, sizes) * scale
    inside = list(inside_rows(place, info, variants))
    tile = best_tile(jnp.zeros((HALF, LANES), jnp.float32), 0, sums, inside)
    lane = lax.broadcasted_iota(jnp.int32, (HALF, LANES), 1)
    for n, mask in enumerate(inside):
        v = jnp.abs(sums[48 + n : 49 + n])
        best = jnp.max(jnp.where(mask, v, 0.0), axis=1, keepdims=True)
        tile = jnp.where(lane == 96 + n, best, tile)
    out[...] = tile


def maxima_kernel(place, info, aux, tile, own, m1, m2, m3, out):
    variants = own.shape[1]
    means = [aux[1 + q : 2 + q, :] for q in range(3)]
    sizes = [aux[4 + q : 5 + q, :] for q in range(3)]
    sums = added(own, (m1, m2, m3), means, sizes) * aux[0:1, :]
    tile = best_tile(tile[...], 1, sums, inside_rows(place, info, variants))
    lane = lax.broadcasted_iota(jnp.int32, (HALF, LANES), 1)
    row = lax.broadcasted_iota(jnp.int32, (HALF, LANES), 0)
    keep = ((lane < 96) & (lane % HALF == row)) | ((lane >= 96) & (row == 0))
    line = jnp.sum(jnp.where(keep, tile, 0.0), axis=0, keepdims=True)
    for i in range(out.shape[0] // HALF):
        out[i * HALF : (i + 1) * HALF, :] = jnp.broadcast_to(line, (HALF, LANES))


def final_kernel(place, order, parts, out, observed, store):
    shards = HALF
    owners = parts.shape[0] // shards
    block = lambda o: parts[o * shards : (o + 1) * shards, :]
    width = 2 * HALF
    for o in range(owners):
        best = block(o)
        if o > 0:
            best = jnp.maximum(best, pltpu.roll(block(o - 1), LANES - 2 * width, 1))
        if o < owners - 1:
            best = jnp.maximum(best, pltpu.roll(block(o + 1), 2 * width, 1))
        store[2 * o] = best
        store[2 * o + 1] = pltpu.roll(best, LANES - width, 1)
    g = place[0]
    zero = jnp.zeros((shards, LANES), jnp.float32)
    tails = [zero, zero]
    for i in range(2 * owners):
        value = store[order[i]]
        for k in range(2):
            tails[k] = jnp.where(i >= 2 * g + k, jnp.maximum(tails[k], value), tails[k])
    lane = lax.broadcasted_iota(jnp.int32, (shards, LANES), 1)
    row = lax.broadcasted_iota(jnp.int32, (shards, LANES), 0)
    for k in range(2):
        moved = pltpu.roll(tails[k], LANES - 2 * width, 1)
        moved = pltpu.roll(moved, 0, 1, stride=width, stride_axis=0)
        out[k : k + 1, :] = jnp.sum(
            jnp.where(lane // width == row, moved, 0.0), axis=0, keepdims=True
        )
    part = lambda o: parts[pl.ds(pl.multiple_of(o * shards, shards), shards), :][:1]
    seen = part(g)
    left = pltpu.roll(part(jnp.maximum(g - 1, 0)), LANES - 2, 1)
    right = pltpu.roll(part(jnp.minimum(g + 1, owners - 1)), 2, 1)
    seen = jnp.maximum(seen, jnp.where(g > 0, left, 0.0))
    seen = jnp.maximum(seen, jnp.where(g < owners - 1, right, 0.0))
    observed[...] = seen[:, 98:100]


def call(kernel, outs, args, us, scratch=(), remote=()):
    scalar = [a.size <= 64 for a in args]
    many = isinstance(outs, list)
    made = pl.pallas_call(
        kernel,
        out_shape=tuple(outs) if many else outs,
        in_specs=[
            pl.BlockSpec(memory_space=pltpu.HBM) if i in remote else SM if k else VM
            for i, k in enumerate(scalar)
        ],
        out_specs=tuple([VM] * len(outs)) if many else VM,
        scratch_shapes=scratch,
        compiler_params=pltpu.CompilerParams(vmem_limit_bytes=24 << 20),
        cost_estimate=pl.CostEstimate(flops=int(us * 1e9), bytes_accessed=0, transcendentals=0),
    )
    args = [
        a
        if k
        else pltpu.with_memory_space_constraint(a, pltpu.HBM if i in remote else pltpu.VMEM)
        for i, (a, k) in enumerate(zip(args, scalar))
    ]
    return made(*args)


def shape(dims, kind=jnp.float32):
    return pltpu.VMEM(dims, kind)


def on_device(dosage, expression, perms, windows, order):
    variants, width = dosage.shape
    owners = lax.axis_size("gene")
    shards = 8
    samples = width * shards
    g, z, c = lax.axis_index("gene"), lax.axis_index("z"), lax.axis_index("core")
    place = jnp.stack([g, z, c]).astype(jnp.int32)
    copies = jnp.broadcast_to(expression.T[None], (shards, 2, width))
    every = lax.all_to_all(copies, ("z", "core"), 0, 0, tiled=True)
    mates = [(0, 1), (1, 0)]
    their_perms = lax.ppermute(perms, "core", mates)
    theirs = lax.ppermute(dosage, "core", mates)
    near_perms = call(
        fetch_kernel,
        shape(perms.shape, jnp.int32),
        [perms],
        1,
        [pltpu.SemaphoreType.DMA],
        remote=(0,),
    )
    stat = call(
        moments_kernel,
        shape((8, variants)),
        [dosage],
        2,
        [pltpu.VMEM((2, variants, LANES), jnp.float32)],
    )
    their_stat = lax.ppermute(stat, "core", mates)

    table_shape = shape((2, samples // LANES, TILE, LANES), jnp.bfloat16)
    first, table = call(
        first_kernel,
        [shape((4 * TILE, 2 * width + LANES), jnp.bfloat16), table_shape],
        [place, windows, every, near_perms, their_perms],
        9,
    )
    second = call(
        functools.partial(later_kernel, 1),
        shape((4 * TILE, 2 * width), jnp.bfloat16),
        [place, near_perms, their_perms, table],
        8,
    )
    ahead = [(i, (i + 1) % owners) for i in range(owners)]
    back = [(b, a) for a, b in ahead]
    sums = []
    for h, own in enumerate((first, second)):
        left = lax.ppermute(own, "gene", ahead)
        right = lax.ppermute(own, "gene", back)
        depth, deep = (56, 64) if h == 0 else (48, 48)
        outs = [shape((depth, variants))] + [shape((deep, variants + LANES), jnp.int16)] * 3
        own, *parts = call(
            functools.partial(sums_kernel, h),
            outs + ([shape((8, LANES))] if h == 0 else []),
            [left, own, right, dosage, theirs, stat, their_stat],
            2,
        )
        if h == 0:
            info = parts.pop()
        group = [own]
        for k in range(1, 4):
            group.append(lax.ppermute(parts[k - 1], "z", [(i, (i + k) % 4) for i in range(4)]))
        sums.append(group)
    tile, aux = call(
        functools.partial(early_kernel, samples),
        [shape((HALF, LANES)), shape((8, variants))],
        [place, info, stat, their_stat, *sums[0]],
        1,
    )
    everyone = owners * shards
    lines = call(maxima_kernel, shape((everyone, LANES)), [place, info, aux, tile, *sums[1]], 2)
    lines = lax.all_to_all(
        lines.reshape(everyone, 1, LANES), ("gene", "z", "core"), 0, 0, tiled=True
    ).reshape(everyone, LANES)
    successive, observed = call(
        final_kernel,
        [jax.ShapeDtypeStruct((2, LANES), jnp.float32), jax.ShapeDtypeStruct((1, 2), jnp.float32)],
        [place, order, lines],
        2,
        [pltpu.VMEM((2 * owners, HALF, LANES), jnp.float32)],
    )
    return observed.reshape(2), successive


def solution(mesh):
    split = Mesh(mesh.devices.reshape(16, 4, 2), ("gene", "z", "core"))
    samp = ("z", "core")
    placed = (P("gene", samp), P(samp, "gene"), P(None, samp), P("gene", None), P())
    return jax.shard_map(
        on_device,
        mesh=split,
        in_specs=placed,
        out_specs=(P("gene"), P("gene", None)),
        check_vma=False,
    )
```

```python
import functools

import jax
import jax.numpy as jnp
from jax import lax
from jax.experimental import pallas as pl
from jax.experimental.pallas import tpu as pltpu
from jax.sharding import Mesh
from jax.sharding import PartitionSpec as P


epsilon = 1e-06
LANES = 128
TILE = 16
HALF = 8
CHUNKS = 2

VM = pl.BlockSpec(memory_space=pltpu.VMEM)
SM = pl.BlockSpec(memory_space=pltpu.SMEM)


def lane_gather(table, index):
    dims = lax.GatherDimensionNumbers(
        offset_dims=(),
        collapsed_slice_dims=(1,),
        start_index_map=(1,),
        operand_batching_dims=(0,),
        start_indices_batching_dims=(0,),
    )
    return lax.gather(
        table,
        index[..., None],
        dims,
        slice_sizes=(1, 1),
        mode=lax.GatherScatterMode.PROMISE_IN_BOUNDS,
    )


def look_up(chunk, genes, place, perms, theirs, table, out):
    z, c = place[1], place[2]
    table_rows = table.shape[1]
    width = perms.shape[1]

    def step(pair, carry):
        first = []
        for k in range(2):
            d = lax.rem(z + pair * 2 + k, 4) * 2 + c
            first.append(pl.multiple_of(d * 2 * HALF + chunk * HALF, HALF))
        for u in range(2 * width // LANES):
            source = perms if u < width // LANES else theirs
            lane = u % (width // LANES) * LANES
            rows = [source[pl.ds(f, HALF), lane : lane + LANES] for f in first]
            index = jnp.concatenate(rows, axis=0)
            low = (index & (LANES - 1)).astype(jnp.int16)
            high = (index >> 7).astype(jnp.int16)
            found = [jnp.zeros((TILE, LANES), jnp.bfloat16) for _ in genes]
            for r in range(table_rows):
                here = high == jnp.int16(r)
                for n, j in enumerate(genes):
                    found[n] = jnp.where(here, lane_gather(table[j, r], low), found[n])
            for n in range(len(genes)):
                row = pl.multiple_of(n * 2 * TILE + pair * TILE, TILE)
                out[pl.ds(row, TILE), u * LANES : (u + 1) * LANES] = found[n]
        return carry

    lax.fori_loop(0, 2, step, 0)


def lane_sums(rows):
    return lax.dot_general(
        jnp.ones((8, LANES), jnp.float32),
        rows,
        (((1,), (1,)), ((), ())),
        precision=lax.Precision.HIGHEST,
        preferred_element_type=jnp.float32,
    )[:1]


def fetch_kernel(source, out, done):
    copy = pltpu.make_async_copy(source, out, done)
    copy.start()
    copy.wait()


def moments_kernel(dosage, out, sums):
    variants, width = dosage.shape

    def step(i, carry):
        rows = pl.ds(pl.multiple_of(i * LANES, LANES), LANES)
        total = jnp.zeros((LANES, LANES), jnp.float32)
        square = jnp.zeros((LANES, LANES), jnp.float32)
        for k in range(width // LANES):
            v = dosage[rows, k * LANES : (k + 1) * LANES].astype(jnp.float32)
            total = total + v
            square = square + v * v
        sums[0, rows, :] = total
        sums[1, rows, :] = square
        return carry

    lax.fori_loop(0, variants // LANES, step, 0)
    out[...] = jnp.zeros_like(out)
    for j in range(2):
        out[j : j + 1, :] = lane_sums(sums[j])


def first_kernel(place, windows, every, perms, theirs, out, table):
    z, c = place[1], place[2]
    shards, genes, width = every.shape
    samples = shards * width
    own = jnp.concatenate([every[z * 2 + c], every[z * 2 + 1 - c]], axis=1)
    direct = []
    for j in range(genes):
        x = every[:, j, :]
        mean = jnp.sum(x, keepdims=True) / samples
        center = x - mean
        scale = lax.rsqrt(jnp.sum(center * center, keepdims=True) / samples + epsilon)
        scaled = center * scale
        for k in range(shards):
            for i in range(width // LANES):
                piece = scaled[k : k + 1, i * LANES : (i + 1) * LANES]
                table[j, k * (width // LANES) + i] = jnp.broadcast_to(piece, (TILE, LANES)).astype(
                    jnp.bfloat16
                )
        direct.append((own[j : j + 1] - mean) * scale)
    tiles = 2 * width // LANES
    lines = [direct[j][:, t * LANES : (t + 1) * LANES] for j in range(genes) for t in range(tiles)]
    lane = lax.broadcasted_iota(jnp.int32, (1, LANES), 1)
    for d in range(2):
        line = jnp.zeros((1, LANES), jnp.float32)
        for j in range(genes):
            for b in range(2):
                w = windows[j, b]
                digit = (w & 127) if d else (w >> 7)
                line = jnp.where(lane == j * 2 + b, digit.astype(jnp.float32), line)
        lines.append(line)
    lines.append(jnp.zeros((4 * TILE - len(lines), LANES), jnp.float32))
    out[:, 2 * width :] = jnp.concatenate(lines, axis=0).astype(jnp.bfloat16)
    look_up(0, (0, 1), place, perms, theirs, table, out)


def later_kernel(chunk, place, perms, theirs, table, out):
    look_up(chunk, (0, 1), place, perms, theirs, table, out)


def times(rows, dosage):
    return lax.dot_general(
        rows, dosage, (((1,), (1,)), ((), ())), preferred_element_type=jnp.float32
    )


LEVELS = 32767.0
PARTS = 256.0


def bound_code(largest):
    return jnp.clip(jnp.ceil(largest * PARTS), 1.0, LEVELS)


def coded(values, code):
    scaled = values * (LEVELS * PARTS / code)
    return jnp.clip(jnp.round(scaled), -LEVELS, LEVELS)


def to_int16(values):
    return values.astype(jnp.int32).astype(jnp.int16)


def digits(x):
    whole = jnp.floor(x)
    rest = (x - whole) * 32768.0
    high = jnp.floor(rest)
    return whole, high, jnp.floor((rest - high) * 32768.0)


def undigits(whole, high, low):
    return whole + (high + low * (1.0 / 32768.0)) * (1.0 / 32768.0)


def mean_and_size(total, square, count):
    mean = total / count
    return mean, jnp.sqrt(jnp.maximum(square - total * mean, 0.0) + count * epsilon)


def sums_kernel(count, with_direct, held, *refs):
    blocks = refs[:count]
    dosage, theirs, stat, their_stat = refs[count : count + 4]
    earlier = refs[count + 4 : count + 4 + held]
    own, m1, m2, m3 = refs[count + 4 + held : count + 8 + held]
    start = earlier[0].shape[0] if held else 0
    variants, width = dosage.shape
    stat = stat[...] + their_stat[...]
    rows = jnp.concatenate([block[:, : 2 * width] for block in blocks], axis=0)
    if with_direct:
        tiles = 2 * width // LANES
        extra = [block[:, 2 * width :].astype(jnp.float32) for block in blocks]
        direct = [
            jnp.concatenate([e[j * tiles + t : j * tiles + t + 1] for t in range(tiles)], axis=1)
            for e in extra
            for j in range(2)
        ]
        direct.append(jnp.zeros((TILE - 6, 2 * width), jnp.float32))
        rows = jnp.concatenate([rows, jnp.concatenate(direct, axis=0).astype(jnp.bfloat16)], axis=0)
    both = times(rows[:, :width], dosage[...]) + times(rows[:, width:], theirs[...])
    column = jnp.sum(rows.astype(jnp.float32), axis=1, keepdims=True)
    mean, size = mean_and_size(stat[0:1, :], stat[1:2, :], 2.0 * width)
    got = (both - column * mean) * (1.0 / size)
    column = jnp.broadcast_to(column, (column.shape[0], LANES))
    at = lambda n, kz: slice(n * 2 * TILE + kz * HALF, n * 2 * TILE + (kz + 1) * HALF)
    for n in range(2 * count):
        own[n * HALF : (n + 1) * HALF, :] = both[at(n, 0)]
    largest = jnp.abs(got[at(0, 1)])
    for n in range(2 * count):
        for kz in range(1, 4):
            largest = jnp.maximum(largest, jnp.abs(got[at(n, kz)]))

    def beside(code, columns):
        lane = lax.broadcasted_iota(jnp.int32, columns.shape, 1)
        whole, high, low = digits(columns)
        line = jnp.where(lane == 1, whole, jnp.where(lane == 2, high, low))
        return to_int16(jnp.where(lane == 0, code, line))

    code = bound_code(jnp.max(largest, keepdims=True))
    for message, before in zip((m1, m2, m3), earlier):
        message[:start, :] = before[...]
    for k, message in enumerate((m1, m2, m3)):
        for t in range(count):
            pair = [at(2 * t, k + 1), at(2 * t + 1, k + 1)]
            values = jnp.concatenate([got[p] for p in pair], axis=0)
            columns = jnp.concatenate([column[p] for p in pair], axis=0)
            message[start + t * TILE : start + (t + 1) * TILE, :variants] = to_int16(coded(values, code))
            message[start + t * TILE : start + (t + 1) * TILE, variants:] = beside(code, columns)
    if with_direct:
        spots = slice(4 * count * TILE, 4 * count * TILE + HALF)
        own[48:56, :] = both[spots]
        values, columns = got[spots], column[spots]
        code = bound_code(jnp.max(jnp.abs(values), keepdims=True))
        rest = list(digits(stat[0:1, :]) + digits(stat[1:2, :]))
        rest.append(jnp.zeros((2, variants), jnp.float32))
        tail = to_int16(jnp.concatenate([coded(values, code)] + rest, axis=0))
        side = beside(code, jnp.concatenate([columns, jnp.zeros_like(columns)], axis=0))
        for message in (m1, m2, m3):
            message[48:64, :variants] = tail
            message[48:64, variants:] = side
        info = refs[-1]
        info[...] = jnp.zeros_like(info)
        for o, e in enumerate(extra):
            info[o : o + 1, :] = e[2 * tiles : 2 * tiles + 1] * 128.0 + e[2 * tiles + 1 : 2 * tiles + 2]


def added(owns, messages, means, sizes):
    total = jnp.concatenate([own[...] for own in owns], axis=0)
    rows, variants = total.shape
    for message, mean, size in zip(messages, means, sizes):
        side = message[:rows, variants:].astype(jnp.int32).astype(jnp.float32)
        column = undigits(side[:, 1:2], side[:, 2:3], side[:, 3:4])
        unit = side[:, 0:1] * (1.0 / (LEVELS * PARTS))
        codes = message[:rows, :variants].astype(jnp.int32).astype(jnp.float32)
        total = total + (codes * unit * size + column * mean)
    return total


def inside_rows(place, info, variants):
    index = lax.broadcasted_iota(jnp.int32, (1, variants), 1) + place[0] * variants
    index = index.astype(jnp.float32)
    for o in range(3):
        for j in range(2):
            lo = info[o : o + 1, j * 2 : j * 2 + 1]
            hi = info[o : o + 1, j * 2 + 1 : j * 2 + 2]
            yield (index >= lo) & (index < hi)


def best_tile(tile, h, total, inside):
    lane = lax.broadcasted_iota(jnp.int32, (HALF, LANES), 1)
    for n, mask in enumerate(inside):
        v = jnp.abs(total[n * HALF : (n + 1) * HALF])
        best = jnp.max(jnp.where(mask, v, 0.0), axis=1, keepdims=True)
        tile = jnp.where(lane // HALF == n * CHUNKS + h, best, tile)
    return tile


def early_kernel(samples, place, info, stat, their_stat, own, m1, m2, m3, out, aux):
    variants = own.shape[1]
    count = samples / 4.0
    stat = stat[...] + their_stat[...]
    total, square = stat[0:1, :], stat[1:2, :]
    means, sizes = [], []
    for message in (m1, m2, m3):
        d = message[48:64, :variants].astype(jnp.int32).astype(jnp.float32)
        their_total = undigits(d[8:9], d[9:10], d[10:11])
        their_square = undigits(d[11:12], d[12:13], d[13:14])
        mean, size = mean_and_size(their_total, their_square, count)
        means.append(mean)
        sizes.append(size)
        total = total + their_total
        square = square + their_square
    row_mean = total / samples
    spread = square / samples - row_mean * row_mean + epsilon
    scale = lax.rsqrt(spread * samples)
    aux[0:1, :] = scale
    for q in range(3):
        aux[1 + q : 2 + q, :] = means[q]
        aux[4 + q : 5 + q, :] = sizes[q]
    aux[7:8, :] = jnp.zeros_like(scale)
    sums = added((own,), (m1, m2, m3), means, sizes) * scale
    inside = list(inside_rows(place, info, variants))
    tile = best_tile(jnp.zeros((HALF, LANES), jnp.float32), 0, sums, inside)
    lane = lax.broadcasted_iota(jnp.int32, (HALF, LANES), 1)
    for n, mask in enumerate(inside):
        v = jnp.abs(sums[48 + n : 49 + n])
        best = jnp.max(jnp.where(mask, v, 0.0), axis=1, keepdims=True)
        tile = jnp.where(lane == 96 + n, best, tile)
    out[...] = tile


def maxima_kernel(place, info, aux, tile, near, far, m1, m2, m3, out):
    variants = near.shape[1]
    means = [aux[1 + q : 2 + q, :] for q in range(3)]
    sizes = [aux[4 + q : 5 + q, :] for q in range(3)]
    sums = added((near, far), (m1, m2, m3), means, sizes) * aux[0:1, :]
    tile = best_tile(tile[...], 1, sums, inside_rows(place, info, variants))
    lane = lax.broadcasted_iota(jnp.int32, (HALF, LANES), 1)
    row = lax.broadcasted_iota(jnp.int32, (HALF, LANES), 0)
    keep = ((lane < 96) & (lane % HALF == row)) | ((lane >= 96) & (row == 0))
    line = jnp.sum(jnp.where(keep, tile, 0.0), axis=0, keepdims=True)
    for i in range(out.shape[0] // HALF):
        out[i * HALF : (i + 1) * HALF, :] = jnp.broadcast_to(line, (HALF, LANES))


def final_kernel(place, order, parts, out, observed, store):
    shards = HALF
    owners = parts.shape[0] // shards
    block = lambda o: parts[o * shards : (o + 1) * shards, :]
    width = 2 * HALF
    for o in range(owners):
        best = block(o)
        if o > 0:
            best = jnp.maximum(best, pltpu.roll(block(o - 1), LANES - 2 * width, 1))
        if o < owners - 1:
            best = jnp.maximum(best, pltpu.roll(block(o + 1), 2 * width, 1))
        store[2 * o] = best
        store[2 * o + 1] = pltpu.roll(best, LANES - width, 1)
    g = place[0]
    zero = jnp.zeros((shards, LANES), jnp.float32)
    tails = [zero, zero]
    for i in range(2 * owners):
        value = store[order[i]]
        for k in range(2):
            tails[k] = jnp.where(i >= 2 * g + k, jnp.maximum(tails[k], value), tails[k])
    lane = lax.broadcasted_iota(jnp.int32, (shards, LANES), 1)
    row = lax.broadcasted_iota(jnp.int32, (shards, LANES), 0)
    for k in range(2):
        moved = pltpu.roll(tails[k], LANES - 2 * width, 1)
        moved = pltpu.roll(moved, 0, 1, stride=width, stride_axis=0)
        out[k : k + 1, :] = jnp.sum(
            jnp.where(lane // width == row, moved, 0.0), axis=0, keepdims=True
        )
    part = lambda o: parts[pl.ds(pl.multiple_of(o * shards, shards), shards), :][:1]
    seen = part(g)
    left = pltpu.roll(part(jnp.maximum(g - 1, 0)), LANES - 2, 1)
    right = pltpu.roll(part(jnp.minimum(g + 1, owners - 1)), 2, 1)
    seen = jnp.maximum(seen, jnp.where(g > 0, left, 0.0))
    seen = jnp.maximum(seen, jnp.where(g < owners - 1, right, 0.0))
    observed[...] = seen[:, 98:100]


def call(kernel, outs, args, us, scratch=(), remote=()):
    scalar = [a.size <= 64 for a in args]
    many = isinstance(outs, list)
    made = pl.pallas_call(
        kernel,
        out_shape=tuple(outs) if many else outs,
        in_specs=[
            pl.BlockSpec(memory_space=pltpu.HBM) if i in remote else SM if k else VM
            for i, k in enumerate(scalar)
        ],
        out_specs=tuple([VM] * len(outs)) if many else VM,
        scratch_shapes=scratch,
        compiler_params=pltpu.CompilerParams(vmem_limit_bytes=24 << 20),
        cost_estimate=pl.CostEstimate(flops=int(us * 1e9), bytes_accessed=0, transcendentals=0),
    )
    args = [
        a
        if k
        else pltpu.with_memory_space_constraint(a, pltpu.HBM if i in remote else pltpu.VMEM)
        for i, (a, k) in enumerate(zip(args, scalar))
    ]
    return made(*args)


def shape(dims, kind=jnp.float32):
    return pltpu.VMEM(dims, kind)


def on_device(dosage, expression, perms, windows, order):
    variants, width = dosage.shape
    owners = lax.axis_size("gene")
    shards = 8
    samples = width * shards
    g, z, c = lax.axis_index("gene"), lax.axis_index("z"), lax.axis_index("core")
    place = jnp.stack([g, z, c]).astype(jnp.int32)
    copies = jnp.broadcast_to(expression.T[None], (shards, 2, width))
    every = lax.all_to_all(copies, ("z", "core"), 0, 0, tiled=True)
    mates = [(0, 1), (1, 0)]
    their_perms = lax.ppermute(perms, "core", mates)
    theirs = lax.ppermute(dosage, "core", mates)
    near_perms = call(
        fetch_kernel,
        shape(perms.shape, jnp.int32),
        [perms],
        1,
        [pltpu.SemaphoreType.DMA],
        remote=(0,),
    )
    stat = call(
        moments_kernel,
        shape((8, variants)),
        [dosage],
        2,
        [pltpu.VMEM((2, variants, LANES), jnp.float32)],
    )
    their_stat = lax.ppermute(stat, "core", mates)

    table_shape = shape((2, samples // LANES, TILE, LANES), jnp.bfloat16)
    first, table = call(
        first_kernel,
        [shape((4 * TILE, 2 * width + LANES), jnp.bfloat16), table_shape],
        [place, windows, every, near_perms, their_perms],
        9,
    )
    second = call(
        functools.partial(later_kernel, 1),
        shape((4 * TILE, 2 * width), jnp.bfloat16),
        [place, near_perms, their_perms, table],
        8,
    )
    ahead = [(i, (i + 1) % owners) for i in range(owners)]
    back = [(b, a) for a, b in ahead]
    sums = []
    for h, own in enumerate((first, second)):
        left = lax.ppermute(own, "gene", ahead)
        right = lax.ppermute(own, "gene", back)
        common = [dosage, theirs, stat, their_stat]
        wide = variants + LANES
        codes = lambda rows: [shape((rows, wide), jnp.int16)] * 3
        if h == 0:
            mine, *parts, info = call(
                functools.partial(sums_kernel, 3, True, 0),
                [shape((56, variants)), *codes(64), shape((8, LANES))],
                [left, own, right, *common],
                2,
            )
            group = [mine]
        else:
            near, *parts = call(
                functools.partial(sums_kernel, 2, False, 0),
                [shape((32, variants)), *codes(32)],
                [left, own, *common],
                1,
            )
            far, *parts = call(
                functools.partial(sums_kernel, 1, False, 3),
                [shape((16, variants)), *codes(48)],
                [right, *common, *parts],
                1,
            )
            group = [near, far]
        for k in range(1, 4):
            group.append(lax.ppermute(parts[k - 1], "z", [(i, (i + k) % 4) for i in range(4)]))
        sums.append(group)
    tile, aux = call(
        functools.partial(early_kernel, samples),
        [shape((HALF, LANES)), shape((8, variants))],
        [place, info, stat, their_stat, *sums[0]],
        1,
    )
    everyone = owners * shards
    lines = call(maxima_kernel, shape((everyone, LANES)), [place, info, aux, tile, *sums[1]], 2)
    lines = lax.all_to_all(
        lines.reshape(everyone, 1, LANES), ("gene", "z", "core"), 0, 0, tiled=True
    ).reshape(everyone, LANES)
    successive, observed = call(
        final_kernel,
        [jax.ShapeDtypeStruct((2, LANES), jnp.float32), jax.ShapeDtypeStruct((1, 2), jnp.float32)],
        [place, order, lines],
        2,
        [pltpu.VMEM((2 * owners, HALF, LANES), jnp.float32)],
    )
    return observed.reshape(2), successive


def solution(mesh):
    split = Mesh(mesh.devices.reshape(16, 4, 2), ("gene", "z", "core"))
    samp = ("z", "core")
    placed = (P("gene", samp), P(samp, "gene"), P(None, samp), P("gene", None), P())
    return jax.shard_map(
        on_device,
        mesh=split,
        in_specs=placed,
        out_specs=(P("gene"), P("gene", None)),
        check_vma=False,
    )
```

```python
import functools

import jax
import jax.numpy as jnp
from jax import lax
from jax.experimental import pallas as pl
from jax.experimental.pallas import tpu as pltpu
from jax.sharding import Mesh
from jax.sharding import PartitionSpec as P


epsilon = 1e-06
LANES = 128
TILE = 16
HALF = 8
CHUNKS = 2

VM = pl.BlockSpec(memory_space=pltpu.VMEM)
SM = pl.BlockSpec(memory_space=pltpu.SMEM)


def lane_gather(table, index):
    dims = lax.GatherDimensionNumbers(
        offset_dims=(),
        collapsed_slice_dims=(1,),
        start_index_map=(1,),
        operand_batching_dims=(0,),
        start_indices_batching_dims=(0,),
    )
    return lax.gather(
        table,
        index[..., None],
        dims,
        slice_sizes=(1, 1),
        mode=lax.GatherScatterMode.PROMISE_IN_BOUNDS,
    )


def look_up(chunk, genes, place, perms, theirs, table, out):
    z, c = place[1], place[2]
    table_rows = table.shape[1]
    width = perms.shape[1]

    def step(pair, carry):
        first = []
        for k in range(2):
            d = lax.rem(z + pair * 2 + k, 4) * 2 + c
            first.append(pl.multiple_of(d * 2 * HALF + chunk * HALF, HALF))
        for u in range(2 * width // LANES):
            source = perms if u < width // LANES else theirs
            lane = u % (width // LANES) * LANES
            rows = [source[pl.ds(f, HALF), lane : lane + LANES] for f in first]
            index = jnp.concatenate(rows, axis=0)
            low = (index & (LANES - 1)).astype(jnp.int16)
            high = (index >> 7).astype(jnp.int16)
            found = [jnp.zeros((TILE, LANES), jnp.bfloat16) for _ in genes]
            for r in range(table_rows):
                here = high == jnp.int16(r)
                for n, j in enumerate(genes):
                    found[n] = jnp.where(here, lane_gather(table[j, r], low), found[n])
            for n in range(len(genes)):
                row = pl.multiple_of(n * 2 * TILE + pair * TILE, TILE)
                out[pl.ds(row, TILE), u * LANES : (u + 1) * LANES] = found[n]
        return carry

    lax.fori_loop(0, 2, step, 0)


def lane_sums(rows):
    return lax.dot_general(
        jnp.ones((8, LANES), jnp.float32),
        rows,
        (((1,), (1,)), ((), ())),
        precision=lax.Precision.HIGHEST,
        preferred_element_type=jnp.float32,
    )[:1]


def fetch_kernel(perms, dosage, near, out, kept, sums, done):
    variants, width = dosage.shape
    pieces = variants // LANES
    copies = []
    for i in range(pieces):
        rows = pl.ds(i * LANES, LANES)
        copies.append(pltpu.make_async_copy(dosage.at[rows], kept.at[rows], done.at[i]))
    copies.append(pltpu.make_async_copy(perms, near, done.at[pieces]))
    for copy in copies:
        copy.start()
    for i in range(pieces):
        copies[i].wait()
        rows = slice(i * LANES, (i + 1) * LANES)
        total = jnp.zeros((LANES, LANES), jnp.float32)
        square = jnp.zeros((LANES, LANES), jnp.float32)
        for k in range(width // LANES):
            v = kept[rows, k * LANES : (k + 1) * LANES].astype(jnp.float32)
            total = total + v
            square = square + v * v
        sums[0, rows, :] = total
        sums[1, rows, :] = square
    out[...] = jnp.zeros_like(out)
    for j in range(2):
        out[j : j + 1, :] = lane_sums(sums[j])
    copies[pieces].wait()


def first_kernel(place, windows, every, perms, theirs, out, table):
    z, c = place[1], place[2]
    shards, genes, width = every.shape
    samples = shards * width
    own = jnp.concatenate([every[z * 2 + c], every[z * 2 + 1 - c]], axis=1)
    direct = []
    for j in range(genes):
        x = every[:, j, :]
        mean = jnp.sum(x, keepdims=True) / samples
        center = x - mean
        scale = lax.rsqrt(jnp.sum(center * center, keepdims=True) / samples + epsilon)
        scaled = center * scale
        for k in range(shards):
            for i in range(width // LANES):
                piece = scaled[k : k + 1, i * LANES : (i + 1) * LANES]
                table[j, k * (width // LANES) + i] = jnp.broadcast_to(piece, (TILE, LANES)).astype(
                    jnp.bfloat16
                )
        direct.append((own[j : j + 1] - mean) * scale)
    tiles = 2 * width // LANES
    lines = [direct[j][:, t * LANES : (t + 1) * LANES] for j in range(genes) for t in range(tiles)]
    lane = lax.broadcasted_iota(jnp.int32, (1, LANES), 1)
    for d in range(2):
        line = jnp.zeros((1, LANES), jnp.float32)
        for j in range(genes):
            for b in range(2):
                w = windows[j, b]
                digit = (w & 127) if d else (w >> 7)
                line = jnp.where(lane == j * 2 + b, digit.astype(jnp.float32), line)
        lines.append(line)
    lines.append(jnp.zeros((4 * TILE - len(lines), LANES), jnp.float32))
    out[:, 2 * width :] = jnp.concatenate(lines, axis=0).astype(jnp.bfloat16)
    look_up(0, (0, 1), place, perms, theirs, table, out)


def later_kernel(chunk, place, perms, theirs, table, out):
    look_up(chunk, (0, 1), place, perms, theirs, table, out)


def times(rows, dosage):
    return lax.dot_general(
        rows, dosage, (((1,), (1,)), ((), ())), preferred_element_type=jnp.float32
    )


LEVELS = 32767.0
PARTS = 256.0


def bound_code(largest):
    return jnp.clip(jnp.ceil(largest * PARTS), 1.0, LEVELS)


def coded(values, code):
    scaled = values * (LEVELS * PARTS / code)
    return jnp.clip(jnp.round(scaled), -LEVELS, LEVELS)


def to_int16(values):
    return values.astype(jnp.int32).astype(jnp.int16)


def digits(x):
    whole = jnp.floor(x)
    rest = (x - whole) * 32768.0
    high = jnp.floor(rest)
    return whole, high, jnp.floor((rest - high) * 32768.0)


def undigits(whole, high, low):
    return whole + (high + low * (1.0 / 32768.0)) * (1.0 / 32768.0)


def mean_and_size(total, square, count):
    mean = total / count
    return mean, jnp.sqrt(jnp.maximum(square - total * mean, 0.0) + count * epsilon)


def sums_kernel(count, with_direct, *refs):
    blocks = refs[:count]
    dosage, theirs, stat, their_stat = refs[count : count + 4]
    own, m1, m2, m3 = refs[count + 4 : count + 8]
    variants, width = dosage.shape
    stat = stat[...] + their_stat[...]
    rows = jnp.concatenate([block[:, : 2 * width] for block in blocks], axis=0)
    if with_direct:
        tiles = 2 * width // LANES
        extra = [block[:, 2 * width :].astype(jnp.float32) for block in blocks]
        direct = [
            jnp.concatenate([e[j * tiles + t : j * tiles + t + 1] for t in range(tiles)], axis=1)
            for e in extra
            for j in range(2)
        ]
        direct.append(jnp.zeros((TILE - 6, 2 * width), jnp.float32))
        rows = jnp.concatenate([rows, jnp.concatenate(direct, axis=0).astype(jnp.bfloat16)], axis=0)
    both = times(rows[:, :width], dosage[...]) + times(rows[:, width:], theirs[...])
    column = jnp.sum(rows.astype(jnp.float32), axis=1, keepdims=True)
    mean, size = mean_and_size(stat[0:1, :], stat[1:2, :], 2.0 * width)
    got = (both - column * mean) * (1.0 / size)
    column = jnp.broadcast_to(column, (column.shape[0], LANES))
    at = lambda n, kz: slice(n * 2 * TILE + kz * HALF, n * 2 * TILE + (kz + 1) * HALF)
    for n in range(2 * count):
        own[n * HALF : (n + 1) * HALF, :] = both[at(n, 0)]
    largest = jnp.abs(got[at(0, 1)])
    for n in range(2 * count):
        for kz in range(1, 4):
            largest = jnp.maximum(largest, jnp.abs(got[at(n, kz)]))

    def beside(code, columns):
        lane = lax.broadcasted_iota(jnp.int32, columns.shape, 1)
        whole, high, low = digits(columns)
        line = jnp.where(lane == 1, whole, jnp.where(lane == 2, high, low))
        return to_int16(jnp.where(lane == 0, code, line))

    code = bound_code(jnp.max(largest, keepdims=True))
    for k, message in enumerate((m1, m2, m3)):
        for t in range(count):
            pair = [at(2 * t, k + 1), at(2 * t + 1, k + 1)]
            values = jnp.concatenate([got[p] for p in pair], axis=0)
            columns = jnp.concatenate([column[p] for p in pair], axis=0)
            message[t * TILE : (t + 1) * TILE, :variants] = to_int16(coded(values, code))
            message[t * TILE : (t + 1) * TILE, variants:] = beside(code, columns)
    if with_direct:
        spots = slice(4 * count * TILE, 4 * count * TILE + HALF)
        own[48:56, :] = both[spots]
        values, columns = got[spots], column[spots]
        code = bound_code(jnp.max(jnp.abs(values), keepdims=True))
        rest = list(digits(stat[0:1, :]) + digits(stat[1:2, :]))
        rest.append(jnp.zeros((2, variants), jnp.float32))
        tail = to_int16(jnp.concatenate([coded(values, code)] + rest, axis=0))
        side = beside(code, jnp.concatenate([columns, jnp.zeros_like(columns)], axis=0))
        for message in (m1, m2, m3):
            message[48:64, :variants] = tail
            message[48:64, variants:] = side
        info = refs[-1]
        info[...] = jnp.zeros_like(info)
        for o, e in enumerate(extra):
            info[o : o + 1, :] = e[2 * tiles : 2 * tiles + 1] * 128.0 + e[2 * tiles + 1 : 2 * tiles + 2]


def added(own, messages, means, sizes):
    total = own[...]
    rows, variants = total.shape
    for message, mean, size in zip(messages, means, sizes):
        side = message[:rows, variants:].astype(jnp.int32).astype(jnp.float32)
        column = undigits(side[:, 1:2], side[:, 2:3], side[:, 3:4])
        unit = side[:, 0:1] * (1.0 / (LEVELS * PARTS))
        codes = message[:rows, :variants].astype(jnp.int32).astype(jnp.float32)
        total = total + (codes * unit * size + column * mean)
    return total


def inside_rows(place, info, variants):
    index = lax.broadcasted_iota(jnp.int32, (1, variants), 1) + place[0] * variants
    index = index.astype(jnp.float32)
    for o in range(3):
        for j in range(2):
            lo = info[o : o + 1, j * 2 : j * 2 + 1]
            hi = info[o : o + 1, j * 2 + 1 : j * 2 + 2]
            yield (index >= lo) & (index < hi)


def best_tile(tile, h, total, inside):
    lane = lax.broadcasted_iota(jnp.int32, (HALF, LANES), 1)
    for n, mask in enumerate(inside):
        v = jnp.abs(total[n * HALF : (n + 1) * HALF])
        best = jnp.max(jnp.where(mask, v, 0.0), axis=1, keepdims=True)
        tile = jnp.where(lane // HALF == n * CHUNKS + h, best, tile)
    return tile


def early_kernel(samples, place, info, stat, their_stat, own, m1, m2, m3, out, aux):
    variants = own.shape[1]
    count = samples / 4.0
    stat = stat[...] + their_stat[...]
    total, square = stat[0:1, :], stat[1:2, :]
    means, sizes = [], []
    for message in (m1, m2, m3):
        d = message[48:64, :variants].astype(jnp.int32).astype(jnp.float32)
        their_total = undigits(d[8:9], d[9:10], d[10:11])
        their_square = undigits(d[11:12], d[12:13], d[13:14])
        mean, size = mean_and_size(their_total, their_square, count)
        means.append(mean)
        sizes.append(size)
        total = total + their_total
        square = square + their_square
    row_mean = total / samples
    spread = square / samples - row_mean * row_mean + epsilon
    scale = lax.rsqrt(spread * samples)
    aux[0:1, :] = scale
    for q in range(3):
        aux[1 + q : 2 + q, :] = means[q]
        aux[4 + q : 5 + q, :] = sizes[q]
    aux[7:8, :] = jnp.zeros_like(scale)
    sums = added(own, (m1, m2, m3), means, sizes) * scale
    inside = list(inside_rows(place, info, variants))
    tile = best_tile(jnp.zeros((HALF, LANES), jnp.float32), 0, sums, inside)
    lane = lax.broadcasted_iota(jnp.int32, (HALF, LANES), 1)
    for n, mask in enumerate(inside):
        v = jnp.abs(sums[48 + n : 49 + n])
        best = jnp.max(jnp.where(mask, v, 0.0), axis=1, keepdims=True)
        tile = jnp.where(lane == 96 + n, best, tile)
    out[...] = tile


def maxima_kernel(place, info, aux, tile, own, m1, m2, m3, out):
    variants = own.shape[1]
    means = [aux[1 + q : 2 + q, :] for q in range(3)]
    sizes = [aux[4 + q : 5 + q, :] for q in range(3)]
    sums = added(own, (m1, m2, m3), means, sizes) * aux[0:1, :]
    tile = best_tile(tile[...], 1, sums, inside_rows(place, info, variants))
    lane = lax.broadcasted_iota(jnp.int32, (HALF, LANES), 1)
    row = lax.broadcasted_iota(jnp.int32, (HALF, LANES), 0)
    keep = ((lane < 96) & (lane % HALF == row)) | ((lane >= 96) & (row == 0))
    line = jnp.sum(jnp.where(keep, tile, 0.0), axis=0, keepdims=True)
    for i in range(out.shape[0] // HALF):
        out[i * HALF : (i + 1) * HALF, :] = jnp.broadcast_to(line, (HALF, LANES))


def final_kernel(place, order, parts, out, observed, store):
    shards = HALF
    owners = parts.shape[0] // shards
    block = lambda o: parts[o * shards : (o + 1) * shards, :]
    width = 2 * HALF
    for o in range(owners):
        best = block(o)
        if o > 0:
            best = jnp.maximum(best, pltpu.roll(block(o - 1), LANES - 2 * width, 1))
        if o < owners - 1:
            best = jnp.maximum(best, pltpu.roll(block(o + 1), 2 * width, 1))
        store[2 * o] = best
        store[2 * o + 1] = pltpu.roll(best, LANES - width, 1)
    g = place[0]
    zero = jnp.zeros((shards, LANES), jnp.float32)
    tails = [zero, zero]
    for i in range(2 * owners):
        value = store[order[i]]
        for k in range(2):
            tails[k] = jnp.where(i >= 2 * g + k, jnp.maximum(tails[k], value), tails[k])
    lane = lax.broadcasted_iota(jnp.int32, (shards, LANES), 1)
    row = lax.broadcasted_iota(jnp.int32, (shards, LANES), 0)
    for k in range(2):
        moved = pltpu.roll(tails[k], LANES - 2 * width, 1)
        moved = pltpu.roll(moved, 0, 1, stride=width, stride_axis=0)
        out[k : k + 1, :] = jnp.sum(
            jnp.where(lane // width == row, moved, 0.0), axis=0, keepdims=True
        )
    part = lambda o: parts[pl.ds(pl.multiple_of(o * shards, shards), shards), :][:1]
    seen = part(g)
    left = pltpu.roll(part(jnp.maximum(g - 1, 0)), LANES - 2, 1)
    right = pltpu.roll(part(jnp.minimum(g + 1, owners - 1)), 2, 1)
    seen = jnp.maximum(seen, jnp.where(g > 0, left, 0.0))
    seen = jnp.maximum(seen, jnp.where(g < owners - 1, right, 0.0))
    observed[...] = seen[:, 98:100]


def call(kernel, outs, args, us, scratch=(), remote=()):
    scalar = [a.size <= 64 for a in args]
    many = isinstance(outs, list)
    made = pl.pallas_call(
        kernel,
        out_shape=tuple(outs) if many else outs,
        in_specs=[
            pl.BlockSpec(memory_space=pltpu.HBM) if i in remote else SM if k else VM
            for i, k in enumerate(scalar)
        ],
        out_specs=tuple([VM] * len(outs)) if many else VM,
        scratch_shapes=scratch,
        compiler_params=pltpu.CompilerParams(vmem_limit_bytes=24 << 20),
        cost_estimate=pl.CostEstimate(flops=int(us * 1e9), bytes_accessed=0, transcendentals=0),
    )
    args = [
        a
        if k
        else pltpu.with_memory_space_constraint(a, pltpu.HBM if i in remote else pltpu.VMEM)
        for i, (a, k) in enumerate(zip(args, scalar))
    ]
    return made(*args)


def shape(dims, kind=jnp.float32):
    return pltpu.VMEM(dims, kind)


def on_device(dosage, expression, perms, windows, order):
    variants, width = dosage.shape
    owners = lax.axis_size("gene")
    shards = 8
    samples = width * shards
    g, z, c = lax.axis_index("gene"), lax.axis_index("z"), lax.axis_index("core")
    place = jnp.stack([g, z, c]).astype(jnp.int32)
    copies = jnp.broadcast_to(expression.T[None], (shards, 2, width))
    every = lax.all_to_all(copies, ("z", "core"), 0, 0, tiled=True)
    mates = [(0, 1), (1, 0)]
    their_perms = lax.ppermute(perms, "core", mates)
    theirs = lax.ppermute(dosage, "core", mates)
    near_perms, stat = call(
        fetch_kernel,
        [shape(perms.shape, jnp.int32), shape((8, variants))],
        [perms, dosage],
        2,
        [
            pltpu.VMEM((variants, width), jnp.bfloat16),
            pltpu.VMEM((2, variants, LANES), jnp.float32),
            pltpu.SemaphoreType.DMA((variants // LANES + 1,)),
        ],
        remote=(0, 1),
    )
    their_stat = lax.ppermute(stat, "core", mates)

    table_shape = shape((2, samples // LANES, TILE, LANES), jnp.bfloat16)
    first, table = call(
        first_kernel,
        [shape((4 * TILE, 2 * width + LANES), jnp.bfloat16), table_shape],
        [place, windows, every, near_perms, their_perms],
        9,
    )
    second = call(
        functools.partial(later_kernel, 1),
        shape((4 * TILE, 2 * width), jnp.bfloat16),
        [place, near_perms, their_perms, table],
        8,
    )
    ahead = [(i, (i + 1) % owners) for i in range(owners)]
    back = [(b, a) for a, b in ahead]
    sums = []
    for h, own in enumerate((first, second)):
        left = lax.ppermute(own, "gene", ahead)
        right = lax.ppermute(own, "gene", back)
        common = [dosage, theirs, stat, their_stat]
        wide = variants + LANES
        codes = lambda rows: [shape((rows, wide), jnp.int16)] * 3
        if h == 0:
            mine, *parts, info = call(
                functools.partial(sums_kernel, 3, True),
                [shape((56, variants)), *codes(64), shape((8, LANES))],
                [left, own, right, *common],
                2,
            )
        else:
            mine, *parts = call(
                functools.partial(sums_kernel, 3, False),
                [shape((48, variants)), *codes(48)],
                [left, own, right, *common],
                2,
            )
        group = [mine]
        for k in range(1, 4):
            group.append(lax.ppermute(parts[k - 1], "z", [(i, (i + k) % 4) for i in range(4)]))
        sums.append(group)
    tile, aux = call(
        functools.partial(early_kernel, samples),
        [shape((HALF, LANES)), shape((8, variants))],
        [place, info, stat, their_stat, *sums[0]],
        1,
    )
    everyone = owners * shards
    lines = call(maxima_kernel, shape((everyone, LANES)), [place, info, aux, tile, *sums[1]], 2)
    lines = lax.all_to_all(
        lines.reshape(everyone, 1, LANES), ("gene", "z", "core"), 0, 0, tiled=True
    ).reshape(everyone, LANES)
    successive, observed = call(
        final_kernel,
        [jax.ShapeDtypeStruct((2, LANES), jnp.float32), jax.ShapeDtypeStruct((1, 2), jnp.float32)],
        [place, order, lines],
        2,
        [pltpu.VMEM((2 * owners, HALF, LANES), jnp.float32)],
    )
    return observed.reshape(2), successive


def solution(mesh):
    split = Mesh(mesh.devices.reshape(16, 4, 2), ("gene", "z", "core"))
    samp = ("z", "core")
    placed = (P("gene", samp), P(samp, "gene"), P(None, samp), P("gene", None), P())
    return jax.shard_map(
        on_device,
        mesh=split,
        in_specs=placed,
        out_specs=(P("gene"), P("gene", None)),
        check_vma=False,
    )
```
